256 devices in a mesh: seq: 64 (over z, y, core), grp: 4 (over x).
Axes of the slice: x: 4, y: 4, z: 8, core: 2. Of those that a mesh axis runs over, the one named last changes fastest.
Arguments:
- queries: bfloat16 [4, 8192, 8192], P('grp', 'seq'), may hold values from -48 to 48
- cotangent: bfloat16 [4, 8192, 8192], P('grp', 'seq'), may hold values from -6 to 6
- cache_keys: bfloat16 [32, 128, 8192], P('grp', None, 'seq'), may hold values from -4.5 to 4.5
- cache_values: bfloat16 [32, 128, 8192], P('grp', None, 'seq'), may hold values from -6 to 6
- block_table: int32 [4, 128, 2], P('grp'), may hold values from 0 to 31, as said below
- block_slot: int32 [32], replicated, may hold values from 0 to 31, as said below
Outputs:
- attended: bfloat16 [4, 8192, 8192], P('grp', 'seq')
- grad_queries: bfloat16 [4, 8192, 8192], P('grp', 'seq')
- grad_keys: bfloat16 [32, 128, 8192], P('grp', None, 'seq')
- grad_values: bfloat16 [32, 128, 8192], P('grp', None, 'seq')
The draws below stay inside these ranges and needn't reach their ends.
Inputs may be any that keep to these rules, and one draw needn't show every extreme that they name: `block_table`: the 2 block ids of one group differ. Every number of 0 to 31 appears once; block id b is held in row block_slot[b] of cache_keys and cache_values.
All inputs are finite; a program needn't handle non-finite values.
Results may differ from the reference program's by a relative error of at most 0.009.
Values may be sent and summed in bfloat16 or wider, within the bound.
A program may use at most 192 MiB of HBM per device.

```python
import math
import jax
import jax.numpy as jnp
from jax import lax

HEADS = 64
HEAD_DIM = 128
GROUP = 64
NEIGHBOURS = 2
NEIGH_LEN = 128
WIDTH = 8192
SEQS = 4
LENGTH = 8192
GROUPS = 128
BLOCKS = 32


def table_of(key):
    base = jax.random.fold_in(key, 11)
    first = jax.random.randint(jax.random.fold_in(base, 1), (SEQS, GROUPS, 1), 0, BLOCKS)
    offset = jax.random.randint(jax.random.fold_in(base, 2), (SEQS, GROUPS, 1), 1, BLOCKS)
    second = (first + offset) % BLOCKS
    return jnp.concatenate([first, second], axis=2).astype(jnp.int32)


def slot_of(key):
    return jax.random.permutation(jax.random.fold_in(key, 12), BLOCKS).astype(jnp.int32)


def keys_of(key):
    base = jax.random.fold_in(key, 13)
    raw = jnp.clip(jax.random.normal(base, (BLOCKS, NEIGH_LEN, WIDTH), jnp.float32), -4.5, 4.5)
    return raw


def draw_block_table(key, part):
    return table_of(key)


def draw_block_slot(key, part):
    return slot_of(key)


def draw_cache_keys(key, part):
    return keys_of(key).astype(jnp.bfloat16)


def draw_queries(key, part):
    base = jax.random.fold_in(key, 14)
    raw = jnp.clip(jax.random.normal(base, (SEQS, LENGTH, WIDTH), jnp.float32), -4.5, 4.5)
    return raw.astype(jnp.bfloat16)


def steps_of(rng, extent, shards, smallest, largest):
    factor_of = 1.0
    for dim, shards_of in shards:
        heights = jax.random.uniform(jax.random.fold_in(jax.random.fold_in(rng, 6), dim), (shards_of,), jnp.float32, smallest / len(shards), largest / len(shards))
        factor_of = factor_of * jnp.repeat(jnp.exp(heights), extent[dim] // shards_of).reshape((-1,) + (1,) * (len(extent) - 1 - dim))
    return factor_of


def normal_values(stream_key, extent, width, reach, cuts=(), kind=jnp.bfloat16):
    entries = jax.random.normal(stream_key, extent, jnp.float32) * width
    if len(cuts) > 0:
        entries = steps_of(stream_key, extent, cuts, -0.22, 0.18) * entries
    return jnp.clip(entries, min=-reach, max=reach).astype(kind)


def setup_inputs(seed: int = 0) -> dict:
    streams_of = jax.random.split(jax.random.key(seed), 7)
    return {
        "queries": draw_queries(jax.random.fold_in(streams_of[6], 71), 0),
        "cotangent": normal_values(streams_of[1], (SEQS, LENGTH, WIDTH), 1.0, 6.0, ((0, 4), (1, 64))),
        "cache_keys": draw_cache_keys(jax.random.fold_in(streams_of[6], 71), 0),
        "cache_values": normal_values(streams_of[3], (BLOCKS, NEIGH_LEN, WIDTH), 1.0, 6.0, ((0, 4), (2, 64))),
        "block_table": draw_block_table(jax.random.fold_in(streams_of[6], 71), 0),
        "block_slot": draw_block_slot(jax.random.fold_in(streams_of[6], 71), 0),
    }


def rounded(values):
    return lax.optimization_barrier(values.astype(jnp.bfloat16)).astype(jnp.float32)

def attend_head(query_head, cotan_head, keys_head, values_head, cache_rows):
    groups = query_head.shape[0] // GROUP
    score_scale = 1.0 / math.sqrt(HEAD_DIM)
    query_blocks = query_head.reshape(groups, GROUP, HEAD_DIM).astype(jnp.float32)
    cotan_blocks = cotan_head.reshape(groups, GROUP, HEAD_DIM).astype(jnp.float32)
    near_keys = keys_head[cache_rows].reshape(groups, NEIGHBOURS * NEIGH_LEN, HEAD_DIM).astype(jnp.float32)
    near_values = values_head[cache_rows].reshape(groups, NEIGHBOURS * NEIGH_LEN, HEAD_DIM).astype(jnp.float32)
    scores = jnp.einsum('cqd,ckd->cqk', query_blocks, near_keys) * score_scale
    row_max = lax.optimization_barrier(jnp.max(scores, axis=-1, keepdims=True))
    weights = jnp.exp(scores - row_max)
    prob = weights / lax.optimization_barrier(jnp.sum(weights, axis=-1, keepdims=True))
    prob_low = rounded(prob)
    attended = jnp.einsum('cqk,ckd->cqd', prob_low, near_values).astype(jnp.bfloat16)
    prob_grad = jnp.einsum('cqd,ckd->cqk', cotan_blocks, near_values)
    row_dot = lax.optimization_barrier(jnp.sum(prob * prob_grad, axis=-1, keepdims=True))
    score_grad = rounded(score_scale * prob * (prob_grad - row_dot))
    query_grad = jnp.einsum('cqk,ckd->cqd', score_grad, near_keys).astype(jnp.bfloat16)
    key_terms = jnp.einsum('cqk,cqd->ckd', score_grad, query_blocks).reshape(groups * NEIGHBOURS, NEIGH_LEN, HEAD_DIM)
    value_terms = jnp.einsum('cqk,cqd->ckd', prob_low, cotan_blocks).reshape(groups * NEIGHBOURS, NEIGH_LEN, HEAD_DIM)
    stored = keys_head.shape[0]
    partial_keys = rounded(jax.ops.segment_sum(key_terms, cache_rows, num_segments=stored))
    partial_values = rounded(jax.ops.segment_sum(value_terms, cache_rows, num_segments=stored))
    return (attended.reshape(-1, HEAD_DIM), query_grad.reshape(-1, HEAD_DIM), partial_keys, partial_values)

def reference(queries, cotangent, cache_keys, cache_values, block_table, block_slot):
    stored = cache_keys.shape[0]
    length = queries.shape[1]
    keys_heads = jnp.transpose(cache_keys.reshape(stored, NEIGH_LEN, HEADS, HEAD_DIM), (2, 0, 1, 3))
    values_heads = jnp.transpose(cache_values.reshape(stored, NEIGH_LEN, HEADS, HEAD_DIM), (2, 0, 1, 3))
    attended_list = []
    grad_list = []
    total_keys = jnp.zeros((HEADS, stored, NEIGH_LEN, HEAD_DIM), jnp.float32)
    total_values = jnp.zeros((HEADS, stored, NEIGH_LEN, HEAD_DIM), jnp.float32)
    for sequence in range(queries.shape[0]):
        cache_rows = block_slot[block_table[sequence]].reshape(-1).astype(jnp.int32)
        query_heads = jnp.transpose(queries[sequence].reshape(length, HEADS, HEAD_DIM), (1, 0, 2))
        cotan_heads = jnp.transpose(cotangent[sequence].reshape(length, HEADS, HEAD_DIM), (1, 0, 2))

        def per_head(pieces):
            return attend_head(pieces[0], pieces[1], pieces[2], pieces[3], cache_rows)
        attended, query_grad, partial_keys, partial_values = lax.map(per_head, (query_heads, cotan_heads, keys_heads, values_heads))
        attended_list.append(jnp.transpose(attended, (1, 0, 2)).reshape(length, HEADS * HEAD_DIM))
        grad_list.append(jnp.transpose(query_grad, (1, 0, 2)).reshape(length, HEADS * HEAD_DIM))
        total_keys = total_keys + partial_keys
        total_values = total_values + partial_values
    grad_keys = jnp.transpose(total_keys, (1, 2, 0, 3)).reshape(stored, NEIGH_LEN, HEADS * HEAD_DIM).astype(jnp.bfloat16)
    grad_values = jnp.transpose(total_values, (1, 2, 0, 3)).reshape(stored, NEIGH_LEN, HEADS * HEAD_DIM).astype(jnp.bfloat16)
    return (jnp.stack(attended_list), jnp.stack(grad_list), grad_keys, grad_values)
```

```python
import functools
import math

import jax
import jax.numpy as jnp
from jax import lax
from jax.experimental import pallas as pl
from jax.experimental.pallas import tpu as pltpu
from jax.sharding import PartitionSpec as P

HEAD_DIM = 128
GROUP = 64
NEIGH_LEN = 128
MESH = pl.DeviceIdType.MESH
ZS, YS, CS, XS = 8, 4, 2, 4
SRC = 32
TOKENS = 128
ROWS = 8
STORED = ROWS * XS
ITEMS = SRC * 4
ZERO = ITEMS


def offsets(i):
    return i % 4, (i // 4) % 4, i // 16


def kernel(
    rows_ref, prev_ref, last_ref, q_ref, g_ref, ck_ref, cv_ref,
    out_ref, grad_ref,
    rbuf, obuf, ka, va, kb, vb, tk, tv, dsend, drecv, krelay, bsend, brelay, bfinal,
    in_send, in_recv, out_send, out_recv, own_sem, ag_send, ag_recv, zs_send, zs_recv, rs_send, rs_recv, bz_send, bz_recv,
):
    scale = 1.0 / math.sqrt(HEAD_DIM)
    seq = lax.axis_index("seq")
    x = lax.axis_index("grp")
    z, y, c = seq // (YS * CS), (seq // CS) % YS, seq % CS
    right, left = (x + 1) % XS, (x + XS - 1) % XS

    def at(zz, yy, cc):
        return (zz * YS + yy) * CS + cc

    z_next = at((z + 2 + 4 * c) % ZS, y, c)

    def source(i):
        k, dy, dc = offsets(i)
        return at((z + k + ZS - 1 - c) % ZS, (y + dy) % YS, (c + dc) % CS)

    def dest(i):
        k, dy, dc = offsets(i)
        cc = (c + dc) % CS
        return at((z - k + ZS + 1 + cc) % ZS, (y - dy + YS) % YS, cc)

    def head_of(device, which):
        return (device + which * (ZS // 2) * YS * CS) % (ZS * YS * CS)

    def columns(head):
        return pl.ds(pl.multiple_of(head * HEAD_DIM, HEAD_DIM), HEAD_DIM)

    barrier = pltpu.get_barrier_semaphore()

    def greet(n, carry):
        zz = (z + ZS - 2 + n // (YS * CS)) % ZS
        peer = at(zz, (n // CS) % YS, n % CS)

        @pl.when(peer != seq)
        def _():
            pl.semaphore_signal(barrier, inc=1, device_id=(peer, x), device_id_type=MESH)

        return carry

    lax.fori_loop(0, 5 * YS * CS, greet, 0)
    for o in range(1, XS):
        pl.semaphore_signal(barrier, inc=1, device_id=(seq, (x + o) % XS), device_id_type=MESH)
    pl.semaphore_wait(barrier, 5 * YS * CS - 1 + XS - 1)

    def remote(src, dst, send, recv, device):
        return pltpu.make_async_remote_copy(
            src_ref=src, dst_ref=dst, send_sem=send, recv_sem=recv, device_id=device, device_id_type=MESH
        )

    def block(owner):
        return pl.ds(pl.multiple_of(owner * ROWS, ROWS), ROWS)

    mine = block(x)
    caches = ((ka, va), (kb, vb))

    def gather_first(which, srcs):
        copies = []
        for kv in range(2):
            dst = caches[which][kv].at[mine]
            copies.append(remote(srcs[kv], dst, ag_send.at[which, 0, kv], ag_recv.at[which, 0, kv], (seq, right)))
            copies.append(remote(srcs[kv], dst, ag_send.at[which, 1, kv], ag_recv.at[which, 1, kv], (seq, left)))
        return copies

    def gather_second(which):
        near = caches[which]
        from_left, from_right = near[0].at[block(left)], near[1].at[block(right)]
        return [
            remote(from_left, from_left, ag_send.at[which, 2, 0], ag_recv.at[which, 2, 0], (seq, right)),
            remote(from_right, from_right, ag_send.at[which, 2, 1], ag_recv.at[which, 2, 1], (seq, left)),
        ]

    own = [
        pltpu.make_async_copy(ck_ref, ka.at[mine], own_sem.at[0]),
        pltpu.make_async_copy(cv_ref, va.at[mine], own_sem.at[1]),
    ]
    gather_a = gather_first(0, (ck_ref, cv_ref))
    shift_first = [
        remote(src, krelay.at[kv], zs_send.at[0, kv], zs_recv.at[0, kv], (z_next, x))
        for kv, src in enumerate((ck_ref, cv_ref))
    ]
    shift_second = [
        remote(krelay.at[kv], caches[1][kv].at[mine], zs_send.at[1, kv], zs_recv.at[1, kv], (z_next, x))
        for kv in range(2)
    ]
    for copy in own + shift_first + gather_a:
        copy.start()

    def in_copies(which, i):
        device = dest(i)
        cols = columns(head_of(device, which))
        return [
            (src.at[:, cols], rbuf.at[which, i, n], in_send.at[which, i], in_recv.at[which, i], (device, x))
            for n, src in enumerate((q_ref, g_ref))
        ]

    def send_in(which):
        def step(i, carry):
            here = dest(i) == seq

            @pl.when(here)
            def _():
                for src, dst, _send, recv, _device in in_copies(which, i):
                    pltpu.make_async_copy(src, dst, recv).start()

            @pl.when(jnp.logical_not(here))
            def _():
                for args in in_copies(which, i):
                    remote(*args).start()

            return carry

        lax.fori_loop(0, SRC, step, 0)

    send_in(0)
    for kv in range(2):
        shift_first[kv].wait_recv()
        shift_second[kv].start()
    gather_a2 = gather_second(0)
    for copy in gather_a:
        copy.wait_recv()
    for copy in gather_a2:
        copy.start()
    send_in(1)

    tk[ZERO] = jnp.zeros((HEAD_DIM, NEIGH_LEN), jnp.float32)
    tv[ZERO] = jnp.zeros((HEAD_DIM, NEIGH_LEN), jnp.float32)
    for copy in own:
        copy.wait()
    for copy in gather_a2:
        copy.wait_recv()

    def nt(a, b):
        return lax.dot_general(a, b, (((1,), (1,)), ((), ())), preferred_element_type=jnp.float32)

    def nn(a, b):
        return lax.dot_general(a, b, (((1,), (0,)), ((), ())), preferred_element_type=jnp.float32)

    def tn(a, b):
        return lax.dot_general(a, b, (((0,), (0,)), ((), ())), preferred_element_type=jnp.float32)

    def attend(which, i):
        kref, vref = caches[which]
        first = source(i) * 4
        for g in range(2):
            span = pl.ds(g * GROUP, GROUP)
            r0, r1 = rows_ref[first + 2 * g], rows_ref[first + 2 * g + 1]
            q = rbuf[which, i, 0, span, :]
            ct = rbuf[which, i, 1, span, :]
            keys = jnp.concatenate([kref[r0], kref[r1]], axis=0)
            vals = jnp.concatenate([vref[r0], vref[r1]], axis=0)
            raw = nt(q, keys)
            weights = jnp.exp((raw - jnp.max(raw, axis=-1, keepdims=True)) * scale)
            prob = weights * (1.0 / jnp.sum(weights, axis=-1, keepdims=True))
            low = prob.astype(jnp.bfloat16)
            obuf[which, i, 0, span, :] = nn(low, vals).astype(jnp.bfloat16)
            pg = nt(ct, vals)
            dot = jnp.sum(prob * pg, axis=-1, keepdims=True)
            sg = (scale * prob * (pg - dot)).astype(jnp.bfloat16)
            obuf[which, i, 1, span, :] = nn(sg, keys).astype(jnp.bfloat16)
            kt = tn(q, sg)
            vt = tn(ct, low)
            for j in range(2):
                before = prev_ref[first + 2 * g + j]
                lanes = slice(j * NEIGH_LEN, (j + 1) * NEIGH_LEN)
                tk[i * 4 + 2 * g + j] = tk[before] + kt[:, lanes]
                tv[i * 4 + 2 * g + j] = tv[before] + vt[:, lanes]

    def send_out(which, i):
        device = source(i)
        cols = columns(head_of(seq, which))
        here = device == seq

        @pl.when(here)
        def _():
            pltpu.make_async_copy(obuf.at[which, i], out_ref.at[:, :, cols], out_recv.at[which, i]).start()

        @pl.when(jnp.logical_not(here))
        def _():
            remote(
                obuf.at[which, i], out_ref.at[:, :, cols], out_send.at[which, i], out_recv.at[which, i], (device, x)
            ).start()

    def compute(which, begin, end):
        def step(i, carry):
            pltpu.make_async_copy(obuf.at[which, i], rbuf.at[which, i], in_recv.at[which, i]).wait()
            attend(which, i)

            @pl.when(i > 0)
            def _():
                send_out(which, i - 1)

            return carry

        lax.fori_loop(begin, end, step, 0)

    def reduce_out(which):
        def step(r, carry):
            slot = last_ref[r]
            dsend[which, r // ROWS, 0, r % ROWS] = tk[slot].astype(jnp.bfloat16)
            dsend[which, r // ROWS, 1, r % ROWS] = tv[slot].astype(jnp.bfloat16)
            return carry

        lax.fori_loop(0, STORED, step, 0)
        send_out(which, SRC - 1)
        copies = []
        for o in range(1, XS):
            xd = (x + o) % XS
            copies.append(
                remote(
                    dsend.at[which, xd], drecv.at[which, o - 1], rs_send.at[which, o - 1], rs_recv.at[which, o - 1],
                    (seq, xd),
                )
            )
        for copy in copies:
            copy.start()
        return copies

    def summed(which, kv, r):
        total = dsend[which, x, kv, r].astype(jnp.float32)
        for o in range(XS - 1):
            total = total + drecv[which, o, kv, r].astype(jnp.float32)
        return total

    compute(0, 0, 8)
    for copy in shift_second:
        copy.wait_recv()
    gather_b = gather_first(1, (kb.at[mine], vb.at[mine]))
    for copy in gather_b:
        copy.start()
    compute(0, 8, 20)
    gather_b2 = gather_second(1)
    for copy in gather_b:
        copy.wait_recv()
    for copy in gather_b2:
        copy.start()
    compute(0, 20, SRC)
    scatter_a = reduce_out(0)
    for copy in gather_b2:
        copy.wait_recv()
    compute(1, 0, SRC)
    scatter_b = reduce_out(1)

    for copy in scatter_b:
        copy.wait_recv()

    def far(n, carry):
        kv, r = n // ROWS, n % ROWS
        bsend[kv, r] = summed(1, kv, r).astype(jnp.bfloat16)
        return carry

    lax.fori_loop(0, 2 * ROWS, far, 0)
    back_first = remote(bsend, brelay, bz_send.at[0], bz_recv.at[0], (z_next, x))
    back_second = remote(brelay, bfinal, bz_send.at[1], bz_recv.at[1], (z_next, x))
    back_first.start()
    for copy in scatter_a:
        copy.wait_recv()
    back_first.wait_recv()
    back_second.start()
    back_second.wait_recv()

    def near(n, carry):
        kv, r = n // ROWS, n % ROWS
        total = summed(0, kv, r) + bfinal[kv, r].astype(jnp.float32)
        grad_ref[kv, r] = total.T.astype(jnp.bfloat16)
        return carry

    lax.fori_loop(0, 2 * ROWS, near, 0)

    def drain(which):
        def step(i, carry):
            pltpu.make_async_copy(obuf.at[which, i], out_ref.at[:, :, columns(0)], out_recv.at[which, i]).wait()

            @pl.when(dest(i) != seq)
            def _():
                remote(
                    obuf.at[which, i], rbuf.at[which, i], in_send.at[which, i], in_recv.at[which, i], (dest(i), x)
                ).wait_send()

            @pl.when(source(i) != seq)
            def _():
                remote(
                    obuf.at[which, i], out_ref.at[:, :, columns(0)], out_send.at[which, i], out_recv.at[which, i],
                    (source(i), x),
                ).wait_send()

            return carry

        lax.fori_loop(0, SRC, step, 0)

    for copy in (
        shift_first + shift_second + gather_a + gather_a2 + gather_b + gather_b2 + scatter_a + scatter_b
        + [back_first, back_second]
    ):
        copy.wait_send()
    drain(0)
    drain(1)


def on_device(queries, cotangent, cache_keys, cache_values, block_table, block_slot):
    seq = lax.axis_index("seq")
    z, y, c = seq // (YS * CS), (seq // CS) % YS, seq % CS
    flat = block_table[0].reshape(-1)
    blocks = block_slot.shape[0]
    hit = flat[:, None] == jnp.arange(blocks, dtype=jnp.int32)[None, :]
    rows = jnp.sum(jnp.where(hit, block_slot[None, :], 0), axis=1)
    item = jnp.arange(flat.shape[0], dtype=jnp.int32)
    src = item // 4
    k = (src // (YS * CS) - z + 1 + c + ZS) % ZS
    step = ((src % CS - c + CS) % CS) * 16 + (((src // CS) % YS - y + YS) % YS) * 4 + k
    slot = jnp.where(k < 4, step * 4 + item % 4, -1)
    same = (rows[:, None] == rows[None, :]) & (slot[None, :] < slot[:, None])
    before = jnp.max(jnp.where(same, slot[None, :], -1), axis=1)
    before = jnp.where(before < 0, ZERO, before)
    final = jnp.max(jnp.where(rows[None, :] == jnp.arange(STORED, dtype=jnp.int32)[:, None], slot[None, :], -1), axis=1)
    final = jnp.where(final < 0, ZERO, final)
    smem = pl.BlockSpec(memory_space=pltpu.SMEM)
    hbm = pl.BlockSpec(memory_space=pl.ANY)
    bf16 = jnp.bfloat16
    dma = pltpu.SemaphoreType.DMA
    out, grads = pl.pallas_call(
        kernel,
        out_shape=(
            jax.ShapeDtypeStruct((2, TOKENS, queries.shape[2]), bf16),
            jax.ShapeDtypeStruct((2, ROWS, NEIGH_LEN, HEAD_DIM), bf16),
        ),
        in_specs=[smem, smem, smem, hbm, hbm, hbm, hbm],
        out_specs=(hbm, pl.BlockSpec(memory_space=pltpu.VMEM)),
        scratch_shapes=[
            pltpu.VMEM((2, SRC, 2, TOKENS, HEAD_DIM), bf16),
            pltpu.VMEM((2, SRC, 2, TOKENS, HEAD_DIM), bf16),
            pltpu.VMEM((STORED, NEIGH_LEN, HEAD_DIM), bf16),
            pltpu.VMEM((STORED, NEIGH_LEN, HEAD_DIM), bf16),
            pltpu.VMEM((STORED, NEIGH_LEN, HEAD_DIM), bf16),
            pltpu.VMEM((STORED, NEIGH_LEN, HEAD_DIM), bf16),
            pltpu.VMEM((ITEMS + 1, HEAD_DIM, NEIGH_LEN), jnp.float32),
            pltpu.VMEM((ITEMS + 1, HEAD_DIM, NEIGH_LEN), jnp.float32),
            pltpu.VMEM((2, XS, 2, ROWS, HEAD_DIM, NEIGH_LEN), bf16),
            pltpu.VMEM((2, XS - 1, 2, ROWS, HEAD_DIM, NEIGH_LEN), bf16),
            pltpu.VMEM((2, ROWS, NEIGH_LEN, HEAD_DIM), bf16),
            pltpu.VMEM((2, ROWS, HEAD_DIM, NEIGH_LEN), bf16),
            pltpu.VMEM((2, ROWS, HEAD_DIM, NEIGH_LEN), bf16),
            pltpu.VMEM((2, ROWS, HEAD_DIM, NEIGH_LEN), bf16),
            dma((2, SRC)), dma((2, SRC)), dma((2, SRC)), dma((2, SRC)),
            dma((2,)), dma((2, 3, 2)), dma((2, 3, 2)), dma((2, 2)), dma((2, 2)),
            dma((2, XS - 1)), dma((2, XS - 1)), dma((2,)), dma((2,)),
        ],
        compiler_params=pltpu.CompilerParams(
            collective_id=0, has_side_effects=True, vmem_limit_bytes=60 * 1024 * 1024
        ),
        name="retrieval_attention",
    )(rows, before, final, queries[0], cotangent[0], cache_keys, cache_values)
    return out[0][None], out[1][None], grads[0], grads[1]


def solution(mesh):
    placed = (
        P("grp", "seq", None),
        P("grp", "seq", None),
        P("grp", None, "seq"),
        P("grp", None, "seq"),
        P("grp", None, None),
        P(),
    )
    return jax.shard_map(
        on_device,
        mesh=mesh,
        in_specs=placed,
        out_specs=(
            P("grp", "seq", None),
            P("grp", "seq", None),
            P("grp", None, "seq"),
            P("grp", None, "seq"),
        ),
        check_vma=False,
    )
```

```python
import functools
import math

import jax
import jax.numpy as jnp
from jax import lax
from jax.experimental import pallas as pl
from jax.experimental.pallas import tpu as pltpu
from jax.sharding import PartitionSpec as P

HEAD_DIM = 128
GROUP = 64
NEIGH_LEN = 128
MESH = pl.DeviceIdType.MESH
ZS, YS, CS, XS = 8, 4, 2, 4
SRC = 32
TOKENS = 128
ROWS = 8
STORED = ROWS * XS
ITEMS = SRC * 4
FIRST = 16
ZERO = ITEMS


def offsets(i):
    other = (i + 24) // 32
    n = i * (1 - other) + other * ((i + 16) // 3 - 8)
    return other * (1 + (i + 1) % 3), n % 4, n // 4


def kernel(
    rows_ref, prev_ref, last_ref, q_ref, g_ref, ck_ref, cv_ref,
    out_ref, grad_ref,
    rbuf, obuf, ka, va, kb, vb, tka, tva, tkb, tvb, dsend, dfar, dnear, dsum, dring, krelay, bsend, brelay, bfinal,
    in_send, in_recv, out_send, out_recv, own_sem, ag_send, ag_recv, zs_send, zs_recv, rs_send, rs_recv, bz_send, bz_recv,
):
    scale = 1.0 / math.sqrt(HEAD_DIM)
    seq = lax.axis_index("seq")
    x = lax.axis_index("grp")
    z, y, c = seq // (YS * CS), (seq // CS) % YS, seq % CS
    right, left = (x + 1) % XS, (x + XS - 1) % XS

    def at(zz, yy, cc):
        return (zz * YS + yy) * CS + cc

    z_next = at((z + 2 + 4 * c) % ZS, y, c)

    def source(i):
        j, dy, dc = offsets(i)
        return at((z + (j + 1 + c) % 4 + ZS - 1 - c) % ZS, (y + dy) % YS, (c + dc) % CS)

    def dest(i):
        j, dy, dc = offsets(i)
        cc = (c + dc) % CS
        return at((z - (j + 1 + cc) % 4 + ZS + 1 + cc) % ZS, (y - dy + YS) % YS, cc)

    def head_of(device, which):
        return (device + which * (ZS // 2) * YS * CS) % (ZS * YS * CS)

    def columns(head):
        return pl.ds(pl.multiple_of(head * HEAD_DIM, HEAD_DIM), HEAD_DIM)

    barrier = pltpu.get_barrier_semaphore()

    def greet(n, carry):
        zz = (z + ZS - 2 + n // (YS * CS)) % ZS
        peer = at(zz, (n // CS) % YS, n % CS)

        @pl.when(peer != seq)
        def _():
            pl.semaphore_signal(barrier, inc=1, device_id=(peer, x), device_id_type=MESH)

        return carry

    lax.fori_loop(0, 5 * YS * CS, greet, 0)
    for o in range(1, XS):
        pl.semaphore_signal(barrier, inc=1, device_id=(seq, (x + o) % XS), device_id_type=MESH)
    pl.semaphore_wait(barrier, 5 * YS * CS - 1 + XS - 1)

    def remote(src, dst, send, recv, device):
        return pltpu.make_async_remote_copy(
            src_ref=src, dst_ref=dst, send_sem=send, recv_sem=recv, device_id=device, device_id_type=MESH
        )

    def block(owner):
        return pl.ds(pl.multiple_of(owner * ROWS, ROWS), ROWS)

    mine = block(x)
    caches = ((ka, va), (kb, vb))
    terms = ((tka, tva), (tkb, tvb))

    def gather_first(which, srcs):
        copies = []
        for kv in range(2):
            dst = caches[which][kv].at[mine]
            copies.append(remote(srcs[kv], dst, ag_send.at[which, 0, kv], ag_recv.at[which, 0, kv], (seq, right)))
            copies.append(remote(srcs[kv], dst, ag_send.at[which, 1, kv], ag_recv.at[which, 1, kv], (seq, left)))
        return copies

    def gather_second(which):
        near = caches[which]
        from_left, from_right = near[0].at[block(left)], near[1].at[block(right)]
        return [
            remote(from_left, from_left, ag_send.at[which, 2, 0], ag_recv.at[which, 2, 0], (seq, right)),
            remote(from_right, from_right, ag_send.at[which, 2, 1], ag_recv.at[which, 2, 1], (seq, left)),
        ]

    own = [
        pltpu.make_async_copy(ck_ref, ka.at[mine], own_sem.at[0]),
        pltpu.make_async_copy(cv_ref, va.at[mine], own_sem.at[1]),
    ]
    gather_a = gather_first(0, (ck_ref, cv_ref))
    shift_first = [
        remote(src, krelay.at[kv], zs_send.at[0, kv], zs_recv.at[0, kv], (z_next, x))
        for kv, src in enumerate((ck_ref, cv_ref))
    ]
    shift_second = [
        remote(krelay.at[kv], caches[1][kv].at[mine], zs_send.at[1, kv], zs_recv.at[1, kv], (z_next, x))
        for kv in range(2)
    ]
    for copy in shift_first + gather_a + own:
        copy.start()

    def in_copies(which, i):
        device = dest(i)
        cols = columns(head_of(device, which))
        return [
            (src.at[:, cols], rbuf.at[which, i, n], in_send.at[which, i], in_recv.at[which, i], (device, x))
            for n, src in enumerate((q_ref, g_ref))
        ]

    def send_in(which, begin, end):
        def step(i, carry):
            here = dest(i) == seq

            @pl.when(here)
            def _():
                for src, dst, _send, recv, _device in in_copies(which, i):
                    pltpu.make_async_copy(src, dst, recv).start()

            @pl.when(jnp.logical_not(here))
            def _():
                for args in in_copies(which, i):
                    remote(*args).start()

            return carry

        lax.fori_loop(begin, end, step, 0)

    send_in(0, 0, 8)
    for kv in range(2):
        shift_first[kv].wait_recv()
        shift_second[kv].start()
    send_in(0, 8, FIRST)
    gather_a2 = gather_second(0)
    for copy in gather_a:
        copy.wait_recv()
    for copy in gather_a2:
        copy.start()
    send_in(1, 0, SRC)
    send_in(0, FIRST, SRC)

    for ref in (tka, tva, tkb, tvb):
        ref[ZERO] = jnp.zeros((HEAD_DIM, NEIGH_LEN), jnp.float32)
    for copy in own:
        copy.wait()
    for copy in gather_a2:
        copy.wait_recv()

    def nt(a, b):
        return lax.dot_general(a, b, (((1,), (1,)), ((), ())), preferred_element_type=jnp.float32)

    def nn(a, b):
        return lax.dot_general(a, b, (((1,), (0,)), ((), ())), preferred_element_type=jnp.float32)

    def tn(a, b):
        return lax.dot_general(a, b, (((0,), (0,)), ((), ())), preferred_element_type=jnp.float32)

    def attend(which, i):
        kref, vref = caches[which]
        tk, tv = terms[which]
        first = source(i) * 4
        for g in range(2):
            span = pl.ds(g * GROUP, GROUP)
            r0, r1 = rows_ref[first + 2 * g], rows_ref[first + 2 * g + 1]
            q = rbuf[which, i, 0, span, :]
            ct = rbuf[which, i, 1, span, :]
            keys = jnp.concatenate([kref[r0], kref[r1]], axis=0)
            vals = jnp.concatenate([vref[r0], vref[r1]], axis=0)
            raw = nt(q, keys)
            weights = jnp.exp((raw - jnp.max(raw, axis=-1, keepdims=True)) * scale)
            prob = weights * (1.0 / jnp.sum(weights, axis=-1, keepdims=True))
            low = prob.astype(jnp.bfloat16)
            obuf[which, i, 0, span, :] = nn(low, vals).astype(jnp.bfloat16)
            pg = nt(ct, vals)
            dot = jnp.sum(prob * pg, axis=-1, keepdims=True)
            sg = (scale * prob * (pg - dot)).astype(jnp.bfloat16)
            obuf[which, i, 1, span, :] = nn(sg, keys).astype(jnp.bfloat16)
            kt = tn(q, sg)
            vt = tn(ct, low)
            for j in range(2):
                before = prev_ref[first + 2 * g + j]
                lanes = slice(j * NEIGH_LEN, (j + 1) * NEIGH_LEN)
                tk[i * 4 + 2 * g + j] = tk[before] + kt[:, lanes]
                tv[i * 4 + 2 * g + j] = tv[before] + vt[:, lanes]

    def send_out(which, i):
        device = source(i)
        cols = columns(head_of(seq, which))
        here = device == seq

        @pl.when(here)
        def _():
            pltpu.make_async_copy(obuf.at[which, i], out_ref.at[:, :, cols], out_recv.at[which, i]).start()

        @pl.when(jnp.logical_not(here))
        def _():
            remote(
                obuf.at[which, i], out_ref.at[:, :, cols], out_send.at[which, i], out_recv.at[which, i], (device, x)
            ).start()

    def compute(which, begin, end, first):
        def step(i, carry):
            pltpu.make_async_copy(obuf.at[which, i], rbuf.at[which, i], in_recv.at[which, i]).wait()
            attend(which, i)

            @pl.when(i > first)
            def _():
                send_out(which, i - 1)

            return carry

        lax.fori_loop(begin, end, step, 0)

    def add(refs):
        total = refs[0][...].astype(jnp.float32)
        for ref in refs[1:]:
            total = total + ref[...].astype(jnp.float32)
        return total

    far_owner = (x + 2) % XS
    toward, away = (right, left), (left, right)

    def scatter_first(which):
        tk, tv = terms[which]

        def step(r, carry):
            slot = last_ref[r]
            dsend[which, r // ROWS, 0, r % ROWS] = tk[slot].astype(jnp.bfloat16)
            dsend[which, r // ROWS, 1, r % ROWS] = tv[slot].astype(jnp.bfloat16)
            return carry

        lax.fori_loop(0, STORED, step, 0)
        copies = []
        for kv in range(2):
            copies.append(
                remote(
                    dsend.at[which, far_owner, kv], dfar.at[which, kv], rs_send.at[which, 0, kv], rs_recv.at[which, 0, kv],
                    (seq, toward[kv]),
                )
            )
        for kv in range(2):
            copies.append(
                remote(
                    dsend.at[which, away[kv], kv], dnear.at[which, kv], rs_send.at[which, 1, kv], rs_recv.at[which, 1, kv],
                    (seq, away[kv]),
                )
            )
        return copies

    def scatter_second(which, first_copies):
        copies = []
        for kv in range(2):
            first_copies[kv].wait_recv()

            def step(r, carry, kv=kv):
                dsum[which, kv, r] = add((dsend.at[which, toward[kv], kv, r], dfar.at[which, kv, r])).astype(jnp.bfloat16)
                return carry

            lax.fori_loop(0, ROWS, step, 0)
            copies.append(
                remote(
                    dsum.at[which, kv], dring.at[which, kv], rs_send.at[which, 2, kv], rs_recv.at[which, 2, kv],
                    (seq, toward[kv]),
                )
            )
        return copies

    def summed(which, kv, r):
        return add((dsend.at[which, x, kv, r], dnear.at[which, kv, r], dring.at[which, kv, r]))

    def start(copies):
        for copy in copies:
            copy.start()

    compute(0, 0, 5, 0)
    for copy in shift_second:
        copy.wait_recv()
    gather_b = gather_first(1, (kb.at[mine], vb.at[mine]))
    start(gather_b)
    compute(0, 5, 11, 0)
    gather_b2 = gather_second(1)
    for copy in gather_b:
        copy.wait_recv()
    start(gather_b2)
    compute(0, 11, FIRST, 0)
    for copy in gather_b2:
        copy.wait_recv()
    send_out(0, FIRST - 1)
    compute(1, 0, SRC, 0)
    scatter_b = scatter_first(1)
    start(scatter_b)
    send_out(1, SRC - 1)
    compute(0, FIRST, FIRST + 6, FIRST)
    scatter_b2 = scatter_second(1, scatter_b)
    start(scatter_b2)
    compute(0, FIRST + 6, FIRST + 12, FIRST)
    for copy in scatter_b[2:] + scatter_b2:
        copy.wait_recv()

    def far(n, carry):
        kv, r = n // ROWS, n % ROWS
        bsend[kv, r] = summed(1, kv, r).astype(jnp.bfloat16)
        return carry

    lax.fori_loop(0, 2 * ROWS, far, 0)
    back_first = remote(bsend, brelay, bz_send.at[0], bz_recv.at[0], (z_next, x))
    back_second = remote(brelay, bfinal, bz_send.at[1], bz_recv.at[1], (z_next, x))
    back_first.start()
    compute(0, FIRST + 12, SRC, FIRST)
    scatter_a = scatter_first(0)
    start(scatter_a)
    send_out(0, SRC - 1)
    scatter_a2 = scatter_second(0, scatter_a)
    start(scatter_a2)
    back_first.wait_recv()
    back_second.start()
    for copy in scatter_a[2:] + scatter_a2:
        copy.wait_recv()
    back_second.wait_recv()

    def near(n, carry):
        kv, r = n // ROWS, n % ROWS
        total = summed(0, kv, r) + bfinal[kv, r].astype(jnp.float32)
        grad_ref[kv, r] = total.T.astype(jnp.bfloat16)
        return carry

    lax.fori_loop(0, 2 * ROWS, near, 0)

    def drain(which):
        def step(i, carry):
            pltpu.make_async_copy(obuf.at[which, i], out_ref.at[:, :, columns(0)], out_recv.at[which, i]).wait()

            @pl.when(dest(i) != seq)
            def _():
                remote(
                    obuf.at[which, i], rbuf.at[which, i], in_send.at[which, i], in_recv.at[which, i], (dest(i), x)
                ).wait_send()

            @pl.when(source(i) != seq)
            def _():
                remote(
                    obuf.at[which, i], out_ref.at[:, :, columns(0)], out_send.at[which, i], out_recv.at[which, i],
                    (source(i), x),
                ).wait_send()

            return carry

        lax.fori_loop(0, SRC, step, 0)

    for copy in (
        shift_first + shift_second + gather_a + gather_a2 + gather_b + gather_b2 + scatter_a + scatter_a2 + scatter_b
        + scatter_b2 + [back_first, back_second]
    ):
        copy.wait_send()
    drain(0)
    drain(1)


def on_device(queries, cotangent, cache_keys, cache_values, block_table, block_slot):
    seq = lax.axis_index("seq")
    z, y, c = seq // (YS * CS), (seq // CS) % YS, seq % CS
    flat = block_table[0].reshape(-1)
    blocks = block_slot.shape[0]
    hit = flat[:, None] == jnp.arange(blocks, dtype=jnp.int32)[None, :]
    rows = jnp.sum(jnp.where(hit, block_slot[None, :], 0), axis=1)
    item = jnp.arange(flat.shape[0], dtype=jnp.int32)
    src = item // 4
    k = (src // (YS * CS) - z + 1 + c + ZS) % ZS
    j = (k + 3 - c) % 4
    n = ((src % CS - c + CS) % CS) * YS + ((src // CS) % YS - y + YS) % YS
    step = jnp.where(j == 0, n, 8 + 3 * n + j - 1)
    slot = jnp.where(k < 4, step * 4 + item % 4, -1)
    same = (rows[:, None] == rows[None, :]) & (slot[None, :] < slot[:, None])
    before = jnp.max(jnp.where(same, slot[None, :], -1), axis=1)
    before = jnp.where(before < 0, ZERO, before)
    final = jnp.max(jnp.where(rows[None, :] == jnp.arange(STORED, dtype=jnp.int32)[:, None], slot[None, :], -1), axis=1)
    final = jnp.where(final < 0, ZERO, final)
    smem = pl.BlockSpec(memory_space=pltpu.SMEM)
    hbm = pl.BlockSpec(memory_space=pl.ANY)
    bf16 = jnp.bfloat16
    dma = pltpu.SemaphoreType.DMA
    out, grads = pl.pallas_call(
        kernel,
        out_shape=(
            jax.ShapeDtypeStruct((2, TOKENS, queries.shape[2]), bf16),
            jax.ShapeDtypeStruct((2, ROWS, NEIGH_LEN, HEAD_DIM), bf16),
        ),
        in_specs=[smem, smem, smem, hbm, hbm, hbm, hbm],
        out_specs=(hbm, pl.BlockSpec(memory_space=pltpu.VMEM)),
        scratch_shapes=[
            pltpu.VMEM((2, SRC, 2, TOKENS, HEAD_DIM), bf16),
            pltpu.VMEM((2, SRC, 2, TOKENS, HEAD_DIM), bf16),
            pltpu.VMEM((STORED, NEIGH_LEN, HEAD_DIM), bf16),
            pltpu.VMEM((STORED, NEIGH_LEN, HEAD_DIM), bf16),
            pltpu.VMEM((STORED, NEIGH_LEN, HEAD_DIM), bf16),
            pltpu.VMEM((STORED, NEIGH_LEN, HEAD_DIM), bf16),
            pltpu.VMEM((ITEMS + 1, HEAD_DIM, NEIGH_LEN), jnp.float32),
            pltpu.VMEM((ITEMS + 1, HEAD_DIM, NEIGH_LEN), jnp.float32),
            pltpu.VMEM((ITEMS + 1, HEAD_DIM, NEIGH_LEN), jnp.float32),
            pltpu.VMEM((ITEMS + 1, HEAD_DIM, NEIGH_LEN), jnp.float32),
            pltpu.VMEM((2, XS, 2, ROWS, HEAD_DIM, NEIGH_LEN), bf16),
            pltpu.VMEM((2, 2, ROWS, HEAD_DIM, NEIGH_LEN), bf16),
            pltpu.VMEM((2, 2, ROWS, HEAD_DIM, NEIGH_LEN), bf16),
            pltpu.VMEM((2, 2, ROWS, HEAD_DIM, NEIGH_LEN), bf16),
            pltpu.VMEM((2, 2, ROWS, HEAD_DIM, NEIGH_LEN), bf16),
            pltpu.VMEM((2, ROWS, NEIGH_LEN, HEAD_DIM), bf16),
            pltpu.VMEM((2, ROWS, HEAD_DIM, NEIGH_LEN), bf16),
            pltpu.VMEM((2, ROWS, HEAD_DIM, NEIGH_LEN), bf16),
            pltpu.VMEM((2, ROWS, HEAD_DIM, NEIGH_LEN), bf16),
            dma((2, SRC)), dma((2, SRC)), dma((2, SRC)), dma((2, SRC)),
            dma((2,)), dma((2, 3, 2)), dma((2, 3, 2)), dma((2, 2)), dma((2, 2)),
            dma((2, 3, 2)), dma((2, 3, 2)), dma((2,)), dma((2,)),
        ],
        compiler_params=pltpu.CompilerParams(
            collective_id=0, has_side_effects=True, vmem_limit_bytes=60 * 1024 * 1024
        ),
        name="retrieval_attention",
    )(rows, before, final, queries[0], cotangent[0], cache_keys, cache_values)
    return out[0][None], out[1][None], grads[0], grads[1]


def solution(mesh):
    placed = (
        P("grp", "seq", None),
        P("grp", "seq", None),
        P("grp", None, "seq"),
        P("grp", None, "seq"),
        P("grp", None, None),
        P(),
    )
    return jax.shard_map(
        on_device,
        mesh=mesh,
        in_specs=placed,
        out_specs=(
            P("grp", "seq", None),
            P("grp", "seq", None),
            P("grp", None, "seq"),
            P("grp", None, "seq"),
        ),
        check_vma=False,
    )
```

```python
import functools
import math

import jax
import jax.numpy as jnp
from jax import lax
from jax.experimental import pallas as pl
from jax.experimental.pallas import tpu as pltpu
from jax.sharding import PartitionSpec as P

HEAD_DIM = 128
GROUP = 64
NEIGH_LEN = 128
MESH = pl.DeviceIdType.MESH
ZS, YS, CS, XS = 8, 4, 2, 4
TOKENS = 128
ROWS = 8
STORED = ROWS * XS
PEERS = YS * CS
NEAR, MID, FAR = range(3)
OFFSETS = ((0, -1, -2), (0, -1, 1), (0, 1))
BASE = (0, 24, 48)
STEPS = 64
ZERO = STEPS * 4


def kernel(
    rows_ref, prev_ref, last_ref, q_ref, g_ref, ck_ref, cv_ref,
    out_ref, grad_ref,
    rbuf, obuf, ka, va, km, vm, kf, vf, tk, tv, dsend, dfar, dnear, dring, bsend, bmid, msend, bfinal,
    in_send, in_recv, out_send, out_recv, own_sem, ag_send, ag_recv, zs_send, zs_recv, rs_send, rs_recv, bz_send, bz_recv,
):
    scale = 1.0 / math.sqrt(HEAD_DIM)
    seq = lax.axis_index("seq")
    x = lax.axis_index("grp")
    z, y, c = seq // (YS * CS), (seq // CS) % YS, seq % CS
    right, left = (x + 1) % XS, (x + XS - 1) % XS

    def at(zz, yy, cc):
        return (zz * YS + yy) * CS + cc

    sign = 1 - 2 * c
    z_next, z_back = at((z + 2 * sign + ZS) % ZS, y, c), at((z - 2 * sign + ZS) % ZS, y, c)

    def source(e, n):
        return at((z + e * sign + ZS) % ZS, (y + n % YS) % YS, (c + n // YS) % CS)

    def dest(e, n):
        cc = (c + n // YS) % CS
        return at((z - e * (1 - 2 * cc) + ZS) % ZS, (y - n % YS + YS) % YS, cc)

    def head_of(device, which):
        if which == MID:
            return (device - 2 * (1 - 2 * (device % CS)) * PEERS + ZS * PEERS) % (ZS * PEERS)
        return (device + (which == FAR) * (ZS // 2) * PEERS) % (ZS * PEERS)

    def slot_of(which, e):
        return BASE[which] + OFFSETS[which].index(e) * PEERS

    def columns(head):
        return pl.ds(pl.multiple_of(head * HEAD_DIM, HEAD_DIM), HEAD_DIM)

    barrier = pltpu.get_barrier_semaphore()

    def greet(n, carry):
        zz = (z + ZS - 2 + n // (YS * CS)) % ZS
        peer = at(zz, (n // CS) % YS, n % CS)

        @pl.when(peer != seq)
        def _():
            pl.semaphore_signal(barrier, inc=1, device_id=(peer, x), device_id_type=MESH)

        return carry

    lax.fori_loop(0, 5 * YS * CS, greet, 0)
    for o in range(1, XS):
        pl.semaphore_signal(barrier, inc=1, device_id=(seq, (x + o) % XS), device_id_type=MESH)
    pl.semaphore_wait(barrier, 5 * YS * CS - 1 + XS - 1)

    def remote(src, dst, send, recv, device):
        return pltpu.make_async_remote_copy(
            src_ref=src, dst_ref=dst, send_sem=send, recv_sem=recv, device_id=device, device_id_type=MESH
        )

    def block(owner):
        return pl.ds(pl.multiple_of(owner * ROWS, ROWS), ROWS)

    mine = block(x)
    caches = ((ka, va), (km, vm), (kf, vf))

    def gather_first(which, srcs):
        copies = []
        for kv in range(2):
            dst = caches[which][kv].at[mine]
            copies.append(remote(srcs[kv], dst, ag_send.at[which, 0, kv], ag_recv.at[which, 0, kv], (seq, right)))
            copies.append(remote(srcs[kv], dst, ag_send.at[which, 1, kv], ag_recv.at[which, 1, kv], (seq, left)))
        return copies

    def gather_second(which):
        near = caches[which]
        from_left, from_right = near[0].at[block(left)], near[1].at[block(right)]
        return [
            remote(from_left, from_left, ag_send.at[which, 2, 0], ag_recv.at[which, 2, 0], (seq, right)),
            remote(from_right, from_right, ag_send.at[which, 2, 1], ag_recv.at[which, 2, 1], (seq, left)),
        ]

    own = [
        pltpu.make_async_copy(ck_ref, ka.at[mine], own_sem.at[0]),
        pltpu.make_async_copy(cv_ref, va.at[mine], own_sem.at[1]),
    ]
    def start(copies):
        for copy in copies:
            copy.start()

    def arrive(copies):
        for copy in copies:
            copy.wait_recv()

    gather_a = gather_first(NEAR, (ck_ref, cv_ref))
    shift_first = [
        remote(src, caches[MID][kv].at[mine], zs_send.at[0, kv], zs_recv.at[0, kv], (z_next, x))
        for kv, src in enumerate((ck_ref, cv_ref))
    ]
    shift_second = [
        remote(caches[MID][kv].at[mine], caches[FAR][kv].at[mine], zs_send.at[1, kv], zs_recv.at[1, kv], (z_next, x))
        for kv in range(2)
    ]
    start(shift_first + gather_a + own)

    def in_copies(which, e, n):
        device = dest(e, n)
        cols = columns(head_of(device, which))
        i = slot_of(which, e) + n
        return [
            (src.at[:, cols], rbuf.at[i, m], in_send.at[i], in_recv.at[i], (device, x))
            for m, src in enumerate((q_ref, g_ref))
        ]

    def send_in(which, e):
        def step(n, carry):
            here = dest(e, n) == seq

            @pl.when(here)
            def _():
                for src, dst, _send, recv, _device in in_copies(which, e, n):
                    pltpu.make_async_copy(src, dst, recv).start()

            @pl.when(jnp.logical_not(here))
            def _():
                for args in in_copies(which, e, n):
                    remote(*args).start()

            return carry

        lax.fori_loop(0, PEERS, step, 0)

    send_in(NEAR, 0)
    send_in(MID, 0)
    for kv in range(2):
        shift_first[kv].wait_recv()
        shift_second[kv].start()
    gather_m = gather_first(MID, (km.at[mine], vm.at[mine]))
    start(gather_m)
    send_in(NEAR, -1)
    gather_a2 = gather_second(NEAR)
    arrive(gather_a)
    start(gather_a2)
    for which, e in ((FAR, 0), (FAR, 1), (MID, -1), (MID, 1), (NEAR, -2)):
        send_in(which, e)

    for ref in (tk, tv):
        ref[ZERO] = jnp.zeros((HEAD_DIM, NEIGH_LEN), jnp.float32)
    for copy in own:
        copy.wait()
    arrive(gather_a2)

    def nt(a, b):
        return lax.dot_general(a, b, (((1,), (1,)), ((), ())), preferred_element_type=jnp.float32)

    def nn(a, b):
        return lax.dot_general(a, b, (((1,), (0,)), ((), ())), preferred_element_type=jnp.float32)

    def tn(a, b):
        return lax.dot_general(a, b, (((0,), (0,)), ((), ())), preferred_element_type=jnp.float32)

    def attend(which, e, n):
        kref, vref = caches[which]
        first = source(e, n) * 4
        i = slot_of(which, e) + n
        chain = which * rows_ref.shape[0] + first
        both = range(2)
        spans = [pl.ds(g * GROUP, GROUP) for g in both]
        qs = [rbuf[i, 0, span, :] for span in spans]
        cts = [rbuf[i, 1, span, :] for span in spans]
        near = [[rows_ref[first + 2 * g + j] for j in range(2)] for g in both]
        keys = [jnp.concatenate([kref[r] for r in near[g]], axis=0) for g in both]
        vals = [jnp.concatenate([vref[r] for r in near[g]], axis=0) for g in both]
        raw = [nt(qs[g], keys[g]) for g in both]
        pg = [nt(cts[g], vals[g]) for g in both]
        tops = [jnp.max(raw[g], axis=-1, keepdims=True) for g in both]
        weights = [jnp.exp((raw[g] - tops[g]) * scale) for g in both]
        sums = [jnp.sum(weights[g], axis=-1, keepdims=True) for g in both]
        crossed = [jnp.sum(weights[g] * pg[g], axis=-1, keepdims=True) for g in both]
        shares = [1.0 / sums[g] for g in both]
        prob = [weights[g] * shares[g] for g in both]
        low = [prob[g].astype(jnp.bfloat16) for g in both]
        sg = [(prob[g] * ((pg[g] - crossed[g] * shares[g]) * scale)).astype(jnp.bfloat16) for g in both]
        attended = [nn(low[g], vals[g]) for g in both]
        grads = [nn(sg[g], keys[g]) for g in both]
        vt = [tn(cts[g], low[g]) for g in both]
        kt = [tn(qs[g], sg[g]) for g in both]
        for g in both:
            obuf[i, 0, spans[g], :] = attended[g].astype(jnp.bfloat16)
            obuf[i, 1, spans[g], :] = grads[g].astype(jnp.bfloat16)
        for g in both:
            for j in range(2):
                before = prev_ref[chain + 2 * g + j]
                lanes = slice(j * NEIGH_LEN, (j + 1) * NEIGH_LEN)
                tk[i * 4 + 2 * g + j] = tk[before] + kt[g][:, lanes]
                tv[i * 4 + 2 * g + j] = tv[before] + vt[g][:, lanes]

    def send_out(which, e, n):
        device = source(e, n)
        cols = columns(head_of(seq, which))
        i = slot_of(which, e) + n
        here = device == seq

        @pl.when(here)
        def _():
            pltpu.make_async_copy(obuf.at[i], out_ref.at[:, :, cols], out_recv.at[i]).start()

        @pl.when(jnp.logical_not(here))
        def _():
            remote(obuf.at[i], out_ref.at[:, :, cols], out_send.at[i], out_recv.at[i], (device, x)).start()

    def compute(which, e, begin=0, end=PEERS, held=None):
        def step(n, carry):
            i = slot_of(which, e) + n
            pltpu.make_async_copy(obuf.at[i], rbuf.at[i], in_recv.at[i]).wait()
            attend(which, e, n)

            @pl.when(n > 0)
            def _():
                send_out(which, e, n - 1)

            if held is not None:

                @pl.when(n == 0)
                def _():
                    send_out(held[0], held[1], PEERS - 1)

            return carry

        lax.fori_loop(begin, end, step, 0)

    def add(refs):
        total = refs[0][...].astype(jnp.float32)
        for ref in refs[1:]:
            total = total + ref[...].astype(jnp.float32)
        return total

    far_owner = (x + 2) % XS
    toward, away = (right, left), (left, right)

    def scatter_first(which):
        def step(r, carry):
            slot = last_ref[which * STORED + r]
            dsend[which, r // ROWS, 0, r % ROWS] = tk[slot].astype(jnp.bfloat16)
            dsend[which, r // ROWS, 1, r % ROWS] = tv[slot].astype(jnp.bfloat16)
            return carry

        lax.fori_loop(0, STORED, step, 0)
        copies = []
        for kv in range(2):
            copies.append(
                remote(
                    dsend.at[which, far_owner, kv], dfar.at[which, kv], rs_send.at[which, 0, kv], rs_recv.at[which, 0, kv],
                    (seq, toward[kv]),
                )
            )
        for kv in range(2):
            copies.append(
                remote(
                    dsend.at[which, away[kv], kv], dnear.at[which, kv], rs_send.at[which, 1, kv], rs_recv.at[which, 1, kv],
                    (seq, away[kv]),
                )
            )
        return copies

    def scatter_second(which, first_copies):
        copies = []
        for kv in range(2):
            first_copies[kv].wait_recv()

            def step(r, carry, kv=kv):
                mine_ref = dsend.at[which, toward[kv], kv, r]
                mine_ref[...] = add((mine_ref, dfar.at[which, kv, r])).astype(jnp.bfloat16)
                return carry

            lax.fori_loop(0, ROWS, step, 0)
            copies.append(
                remote(
                    dsend.at[which, toward[kv], kv], dring.at[which, kv], rs_send.at[which, 2, kv], rs_recv.at[which, 2, kv],
                    (seq, toward[kv]),
                )
            )
        return copies

    def summed(which, kv, r):
        return add((dsend.at[which, x, kv, r], dnear.at[which, kv, r], dring.at[which, kv, r]))

    compute(NEAR, 0)
    gather_m2 = gather_second(MID)
    arrive(gather_m)
    start(gather_m2)
    arrive(shift_second)
    gather_f = gather_first(FAR, (kf.at[mine], vf.at[mine]))
    start(gather_f)
    compute(NEAR, -1, held=(NEAR, 0))
    arrive(gather_m2)
    gather_f2 = gather_second(FAR)
    compute(MID, 0, held=(NEAR, -1))
    arrive(gather_f)
    start(gather_f2)
    arrive(gather_f2)
    compute(FAR, 0, held=(MID, 0))
    compute(FAR, 1, held=(FAR, 0))
    scatter_f = scatter_first(FAR)
    start(scatter_f)
    compute(MID, -1, held=(FAR, 1))
    scatter_f2 = scatter_second(FAR, scatter_f)
    start(scatter_f2)
    compute(MID, 1, held=(MID, -1))
    scatter_m = scatter_first(MID)
    start(scatter_m)
    arrive(scatter_f[2:] + scatter_f2)

    def far(n, carry):
        kv, r = n // ROWS, n % ROWS
        bsend[kv, r] = summed(FAR, kv, r).astype(jnp.bfloat16)
        return carry

    lax.fori_loop(0, 2 * ROWS, far, 0)
    back_first = remote(bsend, bmid, bz_send.at[0], bz_recv.at[0], (z_back, x))
    back_second = remote(msend, bfinal, bz_send.at[1], bz_recv.at[1], (z_back, x))
    back_first.start()
    compute(NEAR, -2, held=(MID, 1))
    scatter_m2 = scatter_second(MID, scatter_m)
    start(scatter_m2)
    scatter_a = scatter_first(NEAR)
    start(scatter_a)
    send_out(NEAR, -2, PEERS - 1)
    arrive(scatter_m[2:] + scatter_m2)
    back_first.wait_recv()

    def middle(n, carry):
        kv, r = n // ROWS, n % ROWS
        msend[kv, r] = (summed(MID, kv, r) + bmid[kv, r].astype(jnp.float32)).astype(jnp.bfloat16)
        return carry

    lax.fori_loop(0, 2 * ROWS, middle, 0)
    back_second.start()
    scatter_a2 = scatter_second(NEAR, scatter_a)
    start(scatter_a2)
    arrive(scatter_a[2:] + scatter_a2)
    back_second.wait_recv()

    def near(n, carry):
        kv, r = n // ROWS, n % ROWS
        total = summed(NEAR, kv, r) + bfinal[kv, r].astype(jnp.float32)
        grad_ref[kv, r] = total.T.astype(jnp.bfloat16)
        return carry

    lax.fori_loop(0, 2 * ROWS, near, 0)

    def drain(which, e):
        def step(n, carry):
            i = slot_of(which, e) + n
            pltpu.make_async_copy(obuf.at[i], out_ref.at[:, :, columns(0)], out_recv.at[i]).wait()

            @pl.when(dest(e, n) != seq)
            def _():
                remote(obuf.at[i], rbuf.at[i], in_send.at[i], in_recv.at[i], (dest(e, n), x)).wait_send()

            @pl.when(source(e, n) != seq)
            def _():
                remote(
                    obuf.at[i], out_ref.at[:, :, columns(0)], out_send.at[i], out_recv.at[i], (source(e, n), x)
                ).wait_send()

            return carry

        lax.fori_loop(0, PEERS, step, 0)

    for copy in (
        shift_first + shift_second + gather_a + gather_a2 + gather_m + gather_m2 + gather_f + gather_f2 + scatter_a
        + scatter_a2 + scatter_m + scatter_m2 + scatter_f + scatter_f2 + [back_first, back_second]
    ):
        copy.wait_send()
    for which in (NEAR, MID, FAR):
        for e in OFFSETS[which]:
            drain(which, e)


def on_device(queries, cotangent, cache_keys, cache_values, block_table, block_slot):
    seq = lax.axis_index("seq")
    z, y, c = seq // (YS * CS), (seq // CS) % YS, seq % CS
    flat = block_table[0].reshape(-1)
    blocks = block_slot.shape[0]
    hit = flat[:, None] == jnp.arange(blocks, dtype=jnp.int32)[None, :]
    rows = jnp.sum(jnp.where(hit, block_slot[None, :], 0), axis=1)
    item = jnp.arange(flat.shape[0], dtype=jnp.int32)
    src = item // 4
    away = ((src // PEERS - z) * (1 - 2 * c) + ZS) % ZS
    n = ((src % CS - c + CS) % CS) * YS + ((src // CS) % YS - y + YS) % YS
    slots = []
    for which in (NEAR, MID, FAR):
        slot = jnp.full_like(item, -1)
        for b, e in enumerate(OFFSETS[which]):
            slot = jnp.where(away == e % ZS, (BASE[which] + b * PEERS + n) * 4 + item % 4, slot)
        slots.append(slot)
    slot = jnp.stack(slots)
    same = (rows[:, None] == rows[None, :])[None] & (slot[:, None, :] < slot[:, :, None])
    before = jnp.max(jnp.where(same, slot[:, None, :], -1), axis=2)
    before = jnp.where(before < 0, ZERO, before).reshape(-1)
    owned = (rows[None, :] == jnp.arange(STORED, dtype=jnp.int32)[:, None])[None]
    final = jnp.max(jnp.where(owned, slot[:, None, :], -1), axis=2)
    final = jnp.where(final < 0, ZERO, final).reshape(-1)
    smem = pl.BlockSpec(memory_space=pltpu.SMEM)
    hbm = pl.BlockSpec(memory_space=pl.ANY)
    bf16 = jnp.bfloat16
    dma = pltpu.SemaphoreType.DMA
    out, grads = pl.pallas_call(
        kernel,
        out_shape=(
            jax.ShapeDtypeStruct((2, TOKENS, queries.shape[2]), bf16),
            jax.ShapeDtypeStruct((2, ROWS, NEIGH_LEN, HEAD_DIM), bf16),
        ),
        in_specs=[smem, smem, smem, hbm, hbm, hbm, hbm],
        out_specs=(hbm, pl.BlockSpec(memory_space=pltpu.VMEM)),
        scratch_shapes=[
            pltpu.VMEM((STEPS, 2, TOKENS, HEAD_DIM), bf16),
            pltpu.VMEM((STEPS, 2, TOKENS, HEAD_DIM), bf16),
            *[pltpu.VMEM((STORED, NEIGH_LEN, HEAD_DIM), bf16)] * 6,
            *[pltpu.VMEM((ZERO + 1, HEAD_DIM, NEIGH_LEN), jnp.float32)] * 2,
            pltpu.VMEM((3, XS, 2, ROWS, HEAD_DIM, NEIGH_LEN), bf16),
            *[pltpu.VMEM((3, 2, ROWS, HEAD_DIM, NEIGH_LEN), bf16)] * 3,
            *[pltpu.VMEM((2, ROWS, HEAD_DIM, NEIGH_LEN), bf16)] * 4,
            dma((STEPS,)), dma((STEPS,)), dma((STEPS,)), dma((STEPS,)),
            dma((2,)), dma((3, 3, 2)), dma((3, 3, 2)), dma((2, 2)), dma((2, 2)),
            dma((3, 3, 2)), dma((3, 3, 2)), dma((2,)), dma((2,)),
        ],
        compiler_params=pltpu.CompilerParams(
            collective_id=0, has_side_effects=True, vmem_limit_bytes=67043328
        ),
        name="retrieval_attention",
    )(rows, before, final, queries[0], cotangent[0], cache_keys, cache_values)
    return out[0][None], out[1][None], grads[0], grads[1]


def solution(mesh):
    placed = (
        P("grp", "seq", None),
        P("grp", "seq", None),
        P("grp", None, "seq"),
        P("grp", None, "seq"),
        P("grp", None, None),
        P(),
    )
    return jax.shard_map(
        on_device,
        mesh=mesh,
        in_specs=placed,
        out_specs=(
            P("grp", "seq", None),
            P("grp", "seq", None),
            P("grp", None, "seq"),
            P("grp", None, "seq"),
        ),
        check_vma=False,
    )
```

```python
import functools
import math

import jax
import jax.numpy as jnp
from jax import lax
from jax.experimental import pallas as pl
from jax.experimental.pallas import tpu as pltpu
from jax.sharding import PartitionSpec as P

HEAD_DIM = 128
GROUP = 64
NEIGH_LEN = 128
MESH = pl.DeviceIdType.MESH
ZS, YS, CS, XS = 8, 4, 2, 4
TOKENS = 128
ROWS = 8
STORED = ROWS * XS
PEERS = YS * CS
NEAR, MID, FAR = range(3)
OFFSETS = ((0, -1, -2), (0, -1, 1), (0, 1))
BASE = (0, 24, 48)
STEPS = 64
ZERO = STEPS * 4


def kernel(
    rows_ref, prev_ref, last_ref, q_ref, g_ref, ck_ref, cv_ref,
    out_ref, grad_ref,
    rbuf, obuf, ka, va, km, vm, kf, vf, tk, tv, dsend, dfar, dnear, dring, bsend, bmid, msend, bfinal,
    in_send, in_recv, out_send, out_recv, own_sem, ag_send, ag_recv, zs_send, zs_recv, rs_send, rs_recv, bz_send, bz_recv,
):
    scale = 1.0 / math.sqrt(HEAD_DIM)
    seq = lax.axis_index("seq")
    x = lax.axis_index("grp")
    z, y, c = seq // (YS * CS), (seq // CS) % YS, seq % CS
    right, left = (x + 1) % XS, (x + XS - 1) % XS

    def at(zz, yy, cc):
        return (zz * YS + yy) * CS + cc

    sign = 1 - 2 * c
    z_next, z_back = at((z + 2 * sign + ZS) % ZS, y, c), at((z - 2 * sign + ZS) % ZS, y, c)

    def source(e, n):
        return at((z + e * sign + ZS) % ZS, (y + n % YS) % YS, (c + n // YS) % CS)

    def dest(e, n):
        cc = (c + n // YS) % CS
        return at((z - e * (1 - 2 * cc) + ZS) % ZS, (y - n % YS + YS) % YS, cc)

    def head_of(device, which):
        if which == MID:
            return (device - 2 * (1 - 2 * (device % CS)) * PEERS + ZS * PEERS) % (ZS * PEERS)
        return (device + (which == FAR) * (ZS // 2) * PEERS) % (ZS * PEERS)

    def slot_of(which, e):
        return BASE[which] + OFFSETS[which].index(e) * PEERS

    def columns(head):
        return pl.ds(pl.multiple_of(head * HEAD_DIM, HEAD_DIM), HEAD_DIM)

    barrier = pltpu.get_barrier_semaphore()

    def greet(n, carry):
        zz = (z + ZS - 2 + n // (YS * CS)) % ZS
        peer = at(zz, (n // CS) % YS, n % CS)

        @pl.when(peer != seq)
        def _():
            pl.semaphore_signal(barrier, inc=1, device_id=(peer, x), device_id_type=MESH)

        return carry

    lax.fori_loop(0, 5 * YS * CS, greet, 0)
    for o in range(1, XS):
        pl.semaphore_signal(barrier, inc=1, device_id=(seq, (x + o) % XS), device_id_type=MESH)
    pl.semaphore_wait(barrier, 5 * YS * CS - 1 + XS - 1)

    def remote(src, dst, send, recv, device):
        return pltpu.make_async_remote_copy(
            src_ref=src, dst_ref=dst, send_sem=send, recv_sem=recv, device_id=device, device_id_type=MESH
        )

    def block(owner):
        return pl.ds(pl.multiple_of(owner * ROWS, ROWS), ROWS)

    mine = block(x)
    caches = ((ka, va), (km, vm), (kf, vf))

    def gather_first(which, srcs):
        copies = []
        for kv in range(2):
            dst = caches[which][kv].at[mine]
            copies.append(remote(srcs[kv], dst, ag_send.at[which, 0, kv], ag_recv.at[which, 0, kv], (seq, right)))
            copies.append(remote(srcs[kv], dst, ag_send.at[which, 1, kv], ag_recv.at[which, 1, kv], (seq, left)))
        return copies

    def gather_second(which):
        near = caches[which]
        from_left, from_right = near[0].at[block(left)], near[1].at[block(right)]
        return [
            remote(from_left, from_left, ag_send.at[which, 2, 0], ag_recv.at[which, 2, 0], (seq, right)),
            remote(from_right, from_right, ag_send.at[which, 2, 1], ag_recv.at[which, 2, 1], (seq, left)),
        ]

    own = [
        pltpu.make_async_copy(ck_ref, ka.at[mine], own_sem.at[0]),
        pltpu.make_async_copy(cv_ref, va.at[mine], own_sem.at[1]),
    ]
    def start(copies):
        for copy in copies:
            copy.start()

    def arrive(copies):
        for copy in copies:
            copy.wait_recv()

    gather_a = gather_first(NEAR, (ck_ref, cv_ref))
    shift_first = [
        remote(src, caches[MID][kv].at[mine], zs_send.at[0, kv], zs_recv.at[0, kv], (z_next, x))
        for kv, src in enumerate((ck_ref, cv_ref))
    ]
    shift_second = [
        remote(caches[MID][kv].at[mine], caches[FAR][kv].at[mine], zs_send.at[1, kv], zs_recv.at[1, kv], (z_next, x))
        for kv in range(2)
    ]
    start(shift_first + gather_a + own)

    def in_copies(which, e, n):
        device = dest(e, n)
        cols = columns(head_of(device, which))
        i = slot_of(which, e) + n
        return [
            (src.at[:, cols], rbuf.at[i, m], in_send.at[i], in_recv.at[i], (device, x))
            for m, src in enumerate((q_ref, g_ref))
        ]

    def send_in(which, e):
        def step(n, carry):
            for args in in_copies(which, e, n):
                remote(*args).start()
            return carry

        if e == 0:
            for src, dst, _send, recv, _device in in_copies(which, e, 0):
                pltpu.make_async_copy(src, dst, recv).start()
        lax.fori_loop(1 if e == 0 else 0, PEERS, step, 0)

    send_in(NEAR, 0)
    send_in(MID, 0)
    for kv in range(2):
        shift_first[kv].wait_recv()
        shift_second[kv].start()
    gather_m = gather_first(MID, (km.at[mine], vm.at[mine]))
    start(gather_m)
    send_in(NEAR, -1)
    gather_a2 = gather_second(NEAR)
    arrive(gather_a)
    start(gather_a2)
    for which, e in ((MID, -1), (FAR, 0), (FAR, 1), (MID, 1), (NEAR, -2)):
        send_in(which, e)

    for ref in (tk, tv):
        ref[ZERO] = jnp.zeros((HEAD_DIM, NEIGH_LEN), jnp.float32)
    for copy in own:
        copy.wait()
    arrive(gather_a2)

    def nt(a, b):
        return lax.dot_general(a, b, (((1,), (1,)), ((), ())), preferred_element_type=jnp.float32)

    def nn(a, b):
        return lax.dot_general(a, b, (((1,), (0,)), ((), ())), preferred_element_type=jnp.float32)

    def tn(a, b):
        return lax.dot_general(a, b, (((0,), (0,)), ((), ())), preferred_element_type=jnp.float32)

    def attend(which, e, n):
        kref, vref = caches[which]
        first = source(e, n) * 4
        i = slot_of(which, e) + n
        chain = which * rows_ref.shape[0] + first
        both = range(2)
        spans = [pl.ds(g * GROUP, GROUP) for g in both]
        qs = [rbuf[i, 0, span, :] for span in spans]
        cts = [rbuf[i, 1, span, :] for span in spans]
        near = [[rows_ref[first + 2 * g + j] for j in range(2)] for g in both]
        keys = [jnp.concatenate([kref[r] for r in near[g]], axis=0) for g in both]
        vals = [jnp.concatenate([vref[r] for r in near[g]], axis=0) for g in both]
        raw = [nt(qs[g], keys[g]) for g in both]
        pg = [nt(cts[g], vals[g]) for g in both]
        tops = [jnp.max(raw[g], axis=-1, keepdims=True) for g in both]
        weights = [jnp.exp((raw[g] - tops[g]) * scale) for g in both]
        sums = [jnp.sum(weights[g], axis=-1, keepdims=True) for g in both]
        crossed = [jnp.sum(weights[g] * pg[g], axis=-1, keepdims=True) for g in both]
        shares = [1.0 / sums[g] for g in both]
        prob = [weights[g] * shares[g] for g in both]
        low = [prob[g].astype(jnp.bfloat16) for g in both]
        sg = [(prob[g] * ((pg[g] - crossed[g] * shares[g]) * scale)).astype(jnp.bfloat16) for g in both]
        attended = [nn(low[g], vals[g]) for g in both]
        grads = [nn(sg[g], keys[g]) for g in both]
        vt = [tn(cts[g], low[g]) for g in both]
        kt = [tn(qs[g], sg[g]) for g in both]
        for g in both:
            obuf[i, 0, spans[g], :] = attended[g].astype(jnp.bfloat16)
            obuf[i, 1, spans[g], :] = grads[g].astype(jnp.bfloat16)
        for g in both:
            for j in range(2):
                before = prev_ref[chain + 2 * g + j]
                lanes = slice(j * NEIGH_LEN, (j + 1) * NEIGH_LEN)
                tk[i * 4 + 2 * g + j] = tk[before] + kt[g][:, lanes]
                tv[i * 4 + 2 * g + j] = tv[before] + vt[g][:, lanes]

    def send_out(which, e, n):
        device = source(e, n)
        cols = columns(head_of(seq, which))
        i = slot_of(which, e) + n

        def away():
            remote(obuf.at[i], out_ref.at[:, :, cols], out_send.at[i], out_recv.at[i], (device, x)).start()

        if e != 0:
            away()
            return
        pl.when(n > 0)(away)

        @pl.when(n == 0)
        def _():
            pltpu.make_async_copy(obuf.at[i], out_ref.at[:, :, cols], out_recv.at[i]).start()

    def compute(which, e, begin=0, end=PEERS, held=None):
        def step(n, carry):
            i = slot_of(which, e) + n
            pltpu.make_async_copy(obuf.at[i], rbuf.at[i], in_recv.at[i]).wait()
            attend(which, e, n)

            @pl.when(n > 0)
            def _():
                send_out(which, e, n - 1)

            if held is not None:

                @pl.when(n == 0)
                def _():
                    send_out(held[0], held[1], PEERS - 1)

            return carry

        lax.fori_loop(begin, end, step, 0)

    def add(refs):
        total = refs[0][...].astype(jnp.float32)
        for ref in refs[1:]:
            total = total + ref[...].astype(jnp.float32)
        return total

    far_owner = (x + 2) % XS
    toward, away = (right, left), (left, right)

    def scatter_first(which):
        def step(r, carry):
            slot = last_ref[which * STORED + r]
            dsend[which, r // ROWS, 0, r % ROWS] = tk[slot].astype(jnp.bfloat16)
            dsend[which, r // ROWS, 1, r % ROWS] = tv[slot].astype(jnp.bfloat16)
            return carry

        lax.fori_loop(0, STORED, step, 0)
        copies = []
        for kv in range(2):
            copies.append(
                remote(
                    dsend.at[which, far_owner, kv], dfar.at[which, kv], rs_send.at[which, 0, kv], rs_recv.at[which, 0, kv],
                    (seq, toward[kv]),
                )
            )
        for kv in range(2):
            copies.append(
                remote(
                    dsend.at[which, away[kv], kv], dnear.at[which, kv], rs_send.at[which, 1, kv], rs_recv.at[which, 1, kv],
                    (seq, away[kv]),
                )
            )
        return copies

    def scatter_second(which, first_copies):
        copies = []
        for kv in range(2):
            first_copies[kv].wait_recv()

            def step(r, carry, kv=kv):
                mine_ref = dsend.at[which, toward[kv], kv, r]
                mine_ref[...] = add((mine_ref, dfar.at[which, kv, r])).astype(jnp.bfloat16)
                return carry

            lax.fori_loop(0, ROWS, step, 0)
            copies.append(
                remote(
                    dsend.at[which, toward[kv], kv], dring.at[which, kv], rs_send.at[which, 2, kv], rs_recv.at[which, 2, kv],
                    (seq, toward[kv]),
                )
            )
        return copies

    def summed(which, kv, r):
        return add((dsend.at[which, x, kv, r], dnear.at[which, kv, r], dring.at[which, kv, r]))

    compute(NEAR, 0)
    gather_m2 = gather_second(MID)
    arrive(gather_m)
    start(gather_m2)
    arrive(shift_second)
    gather_f = gather_first(FAR, (kf.at[mine], vf.at[mine]))
    start(gather_f)
    compute(NEAR, -1, held=(NEAR, 0))
    arrive(gather_m2)
    compute(MID, 0, held=(NEAR, -1))
    gather_f2 = gather_second(FAR)
    arrive(gather_f)
    start(gather_f2)
    compute(MID, -1, held=(MID, 0))
    arrive(gather_f2)
    compute(FAR, 0, held=(MID, -1))
    compute(FAR, 1, held=(FAR, 0))
    scatter_f = scatter_first(FAR)
    start(scatter_f)
    compute(MID, 1, 0, 6, held=(FAR, 1))
    scatter_f2 = scatter_second(FAR, scatter_f)
    start(scatter_f2)
    compute(MID, 1, 6, PEERS)
    scatter_m = scatter_first(MID)
    start(scatter_m)
    compute(NEAR, -2, 0, 4, held=(MID, 1))
    arrive(scatter_f[2:] + scatter_f2)

    def far(n, carry):
        kv, r = n // ROWS, n % ROWS
        bsend[kv, r] = summed(FAR, kv, r).astype(jnp.bfloat16)
        return carry

    lax.fori_loop(0, 2 * ROWS, far, 0)
    back_first = remote(bsend, bmid, bz_send.at[0], bz_recv.at[0], (z_back, x))
    back_second = remote(msend, bfinal, bz_send.at[1], bz_recv.at[1], (z_back, x))
    back_first.start()
    compute(NEAR, -2, 4, 6)
    scatter_m2 = scatter_second(MID, scatter_m)
    start(scatter_m2)
    compute(NEAR, -2, 6, PEERS)
    scatter_a = scatter_first(NEAR)
    start(scatter_a)
    send_out(NEAR, -2, PEERS - 1)
    arrive(scatter_m[2:] + scatter_m2)
    back_first.wait_recv()

    def middle(n, carry):
        kv, r = n // ROWS, n % ROWS
        msend[kv, r] = (summed(MID, kv, r) + bmid[kv, r].astype(jnp.float32)).astype(jnp.bfloat16)
        return carry

    lax.fori_loop(0, 2 * ROWS, middle, 0)
    back_second.start()
    scatter_a2 = scatter_second(NEAR, scatter_a)
    start(scatter_a2)

    def drain(which, e):
        def sent(n, carry):
            i = slot_of(which, e) + n
            pltpu.make_async_copy(obuf.at[i], rbuf.at[i], in_send.at[i]).wait()
            pltpu.make_async_copy(obuf.at[i], rbuf.at[i], out_send.at[i]).wait()
            return carry

        def came(n, carry):
            i = slot_of(which, e) + n
            pltpu.make_async_copy(obuf.at[i], rbuf.at[i], out_recv.at[i]).wait()
            return carry

        lax.fori_loop(1 if e == 0 else 0, PEERS, sent, 0)
        lax.fori_loop(0, PEERS, came, 0)

    drain(NEAR, 0)
    drain(NEAR, -1)
    arrive(scatter_a[2:] + scatter_a2)
    for which, e in ((MID, 0), (MID, -1), (FAR, 0), (FAR, 1)):
        drain(which, e)
    back_second.wait_recv()

    def near(n, carry):
        kv, r = n // ROWS, n % ROWS
        total = summed(NEAR, kv, r) + bfinal[kv, r].astype(jnp.float32)
        grad_ref[kv, r] = total.T.astype(jnp.bfloat16)
        return carry

    lax.fori_loop(0, 2 * ROWS, near, 0)

    for copy in (
        shift_first + shift_second + gather_a + gather_a2 + gather_m + gather_m2 + gather_f + gather_f2 + scatter_a
        + scatter_a2 + scatter_m + scatter_m2 + scatter_f + scatter_f2 + [back_first, back_second]
    ):
        copy.wait_send()
    drain(MID, 1)
    drain(NEAR, -2)


def settle(out_ref, grad_ref, attended_ref, query_ref, keys_ref, values_ref, rows, blocks, in_sem, out_sem):
    moves = []
    for m, dst in enumerate((attended_ref, query_ref)):
        for r in range(4):
            span = pl.ds(r * 32, 32)
            moves.append((out_ref.at[m, span], rows.at[m, span], dst.at[span]))
    for m, dst in enumerate((keys_ref, values_ref)):
        moves.append((grad_ref.at[m], blocks.at[m], dst))
    arriving = [pltpu.make_async_copy(src, mid, in_sem.at[n]) for n, (src, mid, _dst) in enumerate(moves)]
    leaving = [pltpu.make_async_copy(mid, dst, out_sem.at[n]) for n, (_src, mid, dst) in enumerate(moves)]
    for copy in arriving:
        copy.start()
    for first, second in zip(arriving, leaving):
        first.wait()
        second.start()
    for copy in leaving:
        copy.wait()


def on_device(queries, cotangent, cache_keys, cache_values, block_table, block_slot):
    seq = lax.axis_index("seq")
    z, y, c = seq // (YS * CS), (seq // CS) % YS, seq % CS
    flat = block_table[0].reshape(-1)
    blocks = block_slot.shape[0]
    hit = flat[:, None] == jnp.arange(blocks, dtype=jnp.int32)[None, :]
    rows = jnp.sum(jnp.where(hit, block_slot[None, :], 0), axis=1)
    item = jnp.arange(flat.shape[0], dtype=jnp.int32)
    src = item // 4
    away = ((src // PEERS - z) * (1 - 2 * c) + ZS) % ZS
    n = ((src % CS - c + CS) % CS) * YS + ((src // CS) % YS - y + YS) % YS
    slots = []
    for which in (NEAR, MID, FAR):
        slot = jnp.full_like(item, -1)
        for b, e in enumerate(OFFSETS[which]):
            slot = jnp.where(away == e % ZS, (BASE[which] + b * PEERS + n) * 4 + item % 4, slot)
        slots.append(slot)
    slot = jnp.stack(slots)
    same = (rows[:, None] == rows[None, :])[None] & (slot[:, None, :] < slot[:, :, None])
    before = jnp.max(jnp.where(same, slot[:, None, :], -1), axis=2)
    before = jnp.where(before < 0, ZERO, before).reshape(-1)
    owned = (rows[None, :] == jnp.arange(STORED, dtype=jnp.int32)[:, None])[None]
    final = jnp.max(jnp.where(owned, slot[:, None, :], -1), axis=2)
    final = jnp.where(final < 0, ZERO, final).reshape(-1)
    smem = pl.BlockSpec(memory_space=pltpu.SMEM)
    hbm = pl.BlockSpec(memory_space=pl.ANY)
    bf16 = jnp.bfloat16
    dma = pltpu.SemaphoreType.DMA
    out, grads = pl.pallas_call(
        kernel,
        out_shape=(
            jax.ShapeDtypeStruct((2, TOKENS, queries.shape[2]), bf16),
            jax.ShapeDtypeStruct((2, ROWS, NEIGH_LEN, HEAD_DIM), bf16),
        ),
        in_specs=[smem, smem, smem, hbm, hbm, hbm, hbm],
        out_specs=(hbm, pl.BlockSpec(memory_space=pltpu.VMEM)),
        scratch_shapes=[
            pltpu.VMEM((STEPS, 2, TOKENS, HEAD_DIM), bf16),
            pltpu.VMEM((STEPS, 2, TOKENS, HEAD_DIM), bf16),
            *[pltpu.VMEM((STORED, NEIGH_LEN, HEAD_DIM), bf16)] * 6,
            *[pltpu.VMEM((ZERO + 1, HEAD_DIM, NEIGH_LEN), jnp.float32)] * 2,
            pltpu.VMEM((3, XS, 2, ROWS, HEAD_DIM, NEIGH_LEN), bf16),
            *[pltpu.VMEM((3, 2, ROWS, HEAD_DIM, NEIGH_LEN), bf16)] * 3,
            *[pltpu.VMEM((2, ROWS, HEAD_DIM, NEIGH_LEN), bf16)] * 4,
            dma((STEPS,)), dma((STEPS,)), dma((STEPS,)), dma((STEPS,)),
            dma((2,)), dma((3, 3, 2)), dma((3, 3, 2)), dma((2, 2)), dma((2, 2)),
            dma((3, 3, 2)), dma((3, 3, 2)), dma((2,)), dma((2,)),
        ],
        compiler_params=pltpu.CompilerParams(
            collective_id=0, has_side_effects=True, vmem_limit_bytes=67043328
        ),
        name="retrieval_attention",
    )(rows, before, final, queries[0], cotangent[0], cache_keys, cache_values)
    attended, query_grad, keys_grad, values_grad = pl.pallas_call(
        settle,
        out_shape=(
            jax.ShapeDtypeStruct(out.shape[1:], bf16),
            jax.ShapeDtypeStruct(out.shape[1:], bf16),
            jax.ShapeDtypeStruct(grads.shape[1:], bf16),
            jax.ShapeDtypeStruct(grads.shape[1:], bf16),
        ),
        in_specs=[hbm, hbm],
        out_specs=(hbm,) * 4,
        scratch_shapes=[pltpu.VMEM(out.shape, bf16), pltpu.VMEM(grads.shape, bf16), dma((10,)), dma((10,))],
        compiler_params=pltpu.CompilerParams(vmem_limit_bytes=67043328),
        name="settle",
    )(out, grads)
    return attended[None], query_grad[None], keys_grad, values_grad


def solution(mesh):
    placed = (
        P("grp", "seq", None),
        P("grp", "seq", None),
        P("grp", None, "seq"),
        P("grp", None, "seq"),
        P("grp", None, None),
        P(),
    )
    return jax.shard_map(
        on_device,
        mesh=mesh,
        in_specs=placed,
        out_specs=(
            P("grp", "seq", None),
            P("grp", "seq", None),
            P("grp", None, "seq"),
            P("grp", None, "seq"),
        ),
        check_vma=False,
    )
```

```python
import functools
import math

import jax
import jax.numpy as jnp
from jax import lax
from jax.experimental import pallas as pl
from jax.experimental.pallas import tpu as pltpu
from jax.sharding import PartitionSpec as P

HEAD_DIM = 128
GROUP = 64
NEIGH_LEN = 128
MESH = pl.DeviceIdType.MESH
ZS, YS, CS, XS = 8, 4, 2, 4
TOKENS = 128
ROWS = 8
STORED = ROWS * XS
PEERS = YS * CS
NEAR, MID, FAR = range(3)
OFFSETS = ((0, -1, -2), (0, -1, 1), (0, 1))
BASE = (0, 24, 48)
STEPS = 64
ZERO = STEPS * 4


def kernel(
    rows_ref, prev_ref, last_ref, q_ref, g_ref, ck_ref, cv_ref,
    out_ref, grad_ref,
    rbuf, obuf, ka, va, km, vm, kf, vf, tk, tv, dsend, dfar, dnear, dring, bsend, bmid, msend, bfinal,
    in_send, in_recv, out_send, out_recv, own_sem, ag_send, ag_recv, zs_send, zs_recv, rs_send, rs_recv, bz_send, bz_recv,
):
    scale = 1.0 / math.sqrt(HEAD_DIM)
    seq = lax.axis_index("seq")
    x = lax.axis_index("grp")
    z, y, c = seq // (YS * CS), (seq // CS) % YS, seq % CS
    right, left = (x + 1) % XS, (x + XS - 1) % XS

    def at(zz, yy, cc):
        return (zz * YS + yy) * CS + cc

    sign = 1 - 2 * c
    z_next, z_back = at((z + 2 * sign + ZS) % ZS, y, c), at((z - 2 * sign + ZS) % ZS, y, c)

    def source(e, n):
        return at((z + e * sign + ZS) % ZS, (y + n % YS) % YS, (c + n // YS) % CS)

    def dest(e, n):
        cc = (c + n // YS) % CS
        return at((z - e * (1 - 2 * cc) + ZS) % ZS, (y - n % YS + YS) % YS, cc)

    def head_of(device, which):
        if which == MID:
            return (device - 2 * (1 - 2 * (device % CS)) * PEERS + ZS * PEERS) % (ZS * PEERS)
        return (device + (which == FAR) * (ZS // 2) * PEERS) % (ZS * PEERS)

    def slot_of(which, e):
        return BASE[which] + OFFSETS[which].index(e) * PEERS

    def columns(head):
        return pl.ds(pl.multiple_of(head * HEAD_DIM, HEAD_DIM), HEAD_DIM)

    barrier = pltpu.get_barrier_semaphore()

    def greet(n, carry):
        zz = (z + ZS - 2 + n // (YS * CS)) % ZS
        peer = at(zz, (n // CS) % YS, n % CS)

        @pl.when(peer != seq)
        def _():
            pl.semaphore_signal(barrier, inc=1, device_id=(peer, x), device_id_type=MESH)

        return carry

    lax.fori_loop(0, 5 * YS * CS, greet, 0)
    for o in range(1, XS):
        pl.semaphore_signal(barrier, inc=1, device_id=(seq, (x + o) % XS), device_id_type=MESH)
    pl.semaphore_wait(barrier, 5 * YS * CS - 1 + XS - 1)

    def remote(src, dst, send, recv, device):
        return pltpu.make_async_remote_copy(
            src_ref=src, dst_ref=dst, send_sem=send, recv_sem=recv, device_id=device, device_id_type=MESH
        )

    def block(owner):
        return pl.ds(pl.multiple_of(owner * ROWS, ROWS), ROWS)

    mine = block(x)
    caches = ((ka, va), (km, vm), (kf, vf))

    def gather_first(which, srcs):
        copies = []
        for kv in range(2):
            dst = caches[which][kv].at[mine]
            copies.append(remote(srcs[kv], dst, ag_send.at[which, 0, kv], ag_recv.at[which, 0, kv], (seq, right)))
            copies.append(remote(srcs[kv], dst, ag_send.at[which, 1, kv], ag_recv.at[which, 1, kv], (seq, left)))
        return copies

    def gather_second(which):
        near = caches[which]
        from_left, from_right = near[0].at[block(left)], near[1].at[block(right)]
        return [
            remote(from_left, from_left, ag_send.at[which, 2, 0], ag_recv.at[which, 2, 0], (seq, right)),
            remote(from_right, from_right, ag_send.at[which, 2, 1], ag_recv.at[which, 2, 1], (seq, left)),
        ]

    own = [
        pltpu.make_async_copy(ck_ref, ka.at[mine], own_sem.at[0]),
        pltpu.make_async_copy(cv_ref, va.at[mine], own_sem.at[1]),
    ]
    def start(copies):
        for copy in copies:
            copy.start()

    def arrive(copies):
        for copy in copies:
            copy.wait_recv()

    gather_a = gather_first(NEAR, (ck_ref, cv_ref))
    shift_first = [
        remote(src, caches[MID][kv].at[mine], zs_send.at[0, kv], zs_recv.at[0, kv], (z_next, x))
        for kv, src in enumerate((ck_ref, cv_ref))
    ]
    shift_second = [
        remote(caches[MID][kv].at[mine], caches[FAR][kv].at[mine], zs_send.at[1, kv], zs_recv.at[1, kv], (z_next, x))
        for kv in range(2)
    ]
    start(shift_first + gather_a + own)

    def in_copies(which, e, n):
        device = dest(e, n)
        cols = columns(head_of(device, which))
        i = slot_of(which, e) + n
        return [
            (src.at[:, cols], rbuf.at[i, m], in_send.at[i], in_recv.at[i], (device, x))
            for m, src in enumerate((q_ref, g_ref))
        ]

    def send_in(which, e):
        def step(n, carry):
            for args in in_copies(which, e, n):
                remote(*args).start()
            return carry

        if e == 0:
            for src, dst, _send, recv, _device in in_copies(which, e, 0):
                pltpu.make_async_copy(src, dst, recv).start()
        lax.fori_loop(1 if e == 0 else 0, PEERS, step, 0)

    send_in(NEAR, 0)
    send_in(MID, 0)
    for kv in range(2):
        shift_first[kv].wait_recv()
        shift_second[kv].start()
    gather_m = gather_first(MID, (km.at[mine], vm.at[mine]))
    start(gather_m)
    send_in(NEAR, -1)
    gather_a2 = gather_second(NEAR)
    arrive(gather_a)
    start(gather_a2)
    for which, e in ((MID, -1), (FAR, 0), (FAR, 1), (MID, 1), (NEAR, -2)):
        send_in(which, e)

    for ref in (tk, tv):
        ref[ZERO] = jnp.zeros((HEAD_DIM, NEIGH_LEN), jnp.float32)
    for copy in own:
        copy.wait()
    arrive(gather_a2)

    def nt(a, b):
        return lax.dot_general(a, b, (((1,), (1,)), ((), ())), preferred_element_type=jnp.float32)

    def nn(a, b):
        return lax.dot_general(a, b, (((1,), (0,)), ((), ())), preferred_element_type=jnp.float32)

    def tn(a, b):
        return lax.dot_general(a, b, (((0,), (0,)), ((), ())), preferred_element_type=jnp.float32)

    def attend(which, e, steps):
        kref, vref = caches[which]
        firsts = [source(e, n) * 4 for n in steps]
        slots = [slot_of(which, e) + n for n in steps]
        both = range(2 * len(steps))
        at_slot = [(slots[g // 2], pl.ds(g % 2 * GROUP, GROUP)) for g in both]
        qs = [rbuf[i, 0, span, :] for i, span in at_slot]
        cts = [rbuf[i, 1, span, :] for i, span in at_slot]
        near = [[rows_ref[firsts[g // 2] + g % 2 * 2 + j] for j in range(2)] for g in both]
        keys = [jnp.concatenate([kref[r] for r in near[g]], axis=0) for g in both]
        vals = [jnp.concatenate([vref[r] for r in near[g]], axis=0) for g in both]
        raw = [nt(qs[g], keys[g]) for g in both]
        pg = [nt(cts[g], vals[g]) for g in both]
        tops = [jnp.max(raw[g], axis=-1, keepdims=True) for g in both]
        weights = [jnp.exp((raw[g] - tops[g]) * scale) for g in both]
        sums = [jnp.sum(weights[g], axis=-1, keepdims=True) for g in both]
        crossed = [jnp.sum(weights[g] * pg[g], axis=-1, keepdims=True) for g in both]
        shares = [1.0 / sums[g] for g in both]
        prob = [weights[g] * shares[g] for g in both]
        low = [prob[g].astype(jnp.bfloat16) for g in both]
        sg = [(prob[g] * ((pg[g] - crossed[g] * shares[g]) * scale)).astype(jnp.bfloat16) for g in both]
        attended = [nn(low[g], vals[g]) for g in both]
        grads = [nn(sg[g], keys[g]) for g in both]
        vt = [tn(cts[g], low[g]) for g in both]
        kt = [tn(qs[g], sg[g]) for g in both]
        for g, (i, span) in enumerate(at_slot):
            obuf[i, 0, span, :] = attended[g].astype(jnp.bfloat16)
            obuf[i, 1, span, :] = grads[g].astype(jnp.bfloat16)
        for g, (i, _span) in enumerate(at_slot):
            for j in range(2):
                before = prev_ref[which * rows_ref.shape[0] + firsts[g // 2] + g % 2 * 2 + j]
                lanes = slice(j * NEIGH_LEN, (j + 1) * NEIGH_LEN)
                tk[i * 4 + g % 2 * 2 + j] = tk[before] + kt[g][:, lanes]
                tv[i * 4 + g % 2 * 2 + j] = tv[before] + vt[g][:, lanes]

    def send_out(which, e, n):
        device = source(e, n)
        cols = columns(head_of(seq, which))
        i = slot_of(which, e) + n

        def away():
            remote(obuf.at[i], out_ref.at[:, :, cols], out_send.at[i], out_recv.at[i], (device, x)).start()

        if e != 0:
            away()
            return
        pl.when(n > 0)(away)

        @pl.when(n == 0)
        def _():
            pltpu.make_async_copy(obuf.at[i], out_ref.at[:, :, cols], out_recv.at[i]).start()

    def send_pair(which, e, m):
        send_out(which, e, 2 * m)
        send_out(which, e, 2 * m + 1)

    def compute(which, e, begin=0, end=PEERS, held=None):
        def step(m, carry):
            pair = (2 * m, 2 * m + 1)
            for n in pair:
                i = slot_of(which, e) + n
                pltpu.make_async_copy(obuf.at[i], rbuf.at[i], in_recv.at[i]).wait()
            attend(which, e, pair)

            @pl.when(m > 0)
            def _():
                send_pair(which, e, m - 1)

            if held is not None:

                @pl.when(m == 0)
                def _():
                    send_pair(held[0], held[1], PEERS // 2 - 1)

            return carry

        lax.fori_loop(begin // 2, end // 2, step, 0)

    def add(refs):
        total = refs[0][...].astype(jnp.float32)
        for ref in refs[1:]:
            total = total + ref[...].astype(jnp.float32)
        return total

    far_owner = (x + 2) % XS
    toward, away = (right, left), (left, right)

    def scatter_first(which):
        def step(r, carry):
            slot = last_ref[which * STORED + r]
            dsend[which, r // ROWS, 0, r % ROWS] = tk[slot].astype(jnp.bfloat16)
            dsend[which, r // ROWS, 1, r % ROWS] = tv[slot].astype(jnp.bfloat16)
            return carry

        lax.fori_loop(0, STORED, step, 0)
        copies = []
        for kv in range(2):
            copies.append(
                remote(
                    dsend.at[which, far_owner, kv], dfar.at[which, kv], rs_send.at[which, 0, kv], rs_recv.at[which, 0, kv],
                    (seq, toward[kv]),
                )
            )
        for kv in range(2):
            copies.append(
                remote(
                    dsend.at[which, away[kv], kv], dnear.at[which, kv], rs_send.at[which, 1, kv], rs_recv.at[which, 1, kv],
                    (seq, away[kv]),
                )
            )
        return copies

    def scatter_second(which, first_copies):
        copies = []
        for kv in range(2):
            first_copies[kv].wait_recv()

            def step(r, carry, kv=kv):
                mine_ref = dsend.at[which, toward[kv], kv, r]
                mine_ref[...] = add((mine_ref, dfar.at[which, kv, r])).astype(jnp.bfloat16)
                return carry

            lax.fori_loop(0, ROWS, step, 0)
            copies.append(
                remote(
                    dsend.at[which, toward[kv], kv], dring.at[which, kv], rs_send.at[which, 2, kv], rs_recv.at[which, 2, kv],
                    (seq, toward[kv]),
                )
            )
        return copies

    def summed(which, kv, r):
        return add((dsend.at[which, x, kv, r], dnear.at[which, kv, r], dring.at[which, kv, r]))

    compute(NEAR, 0)
    gather_m2 = gather_second(MID)
    arrive(gather_m)
    start(gather_m2)
    arrive(shift_second)
    gather_f = gather_first(FAR, (kf.at[mine], vf.at[mine]))
    start(gather_f)
    compute(NEAR, -1, held=(NEAR, 0))
    arrive(gather_m2)
    compute(MID, 0, held=(NEAR, -1))
    gather_f2 = gather_second(FAR)
    arrive(gather_f)
    start(gather_f2)
    compute(MID, -1, held=(MID, 0))
    arrive(gather_f2)
    compute(FAR, 0, held=(MID, -1))
    compute(FAR, 1, held=(FAR, 0))
    scatter_f = scatter_first(FAR)
    start(scatter_f)
    compute(MID, 1, 0, 6, held=(FAR, 1))
    scatter_f2 = scatter_second(FAR, scatter_f)
    start(scatter_f2)
    compute(MID, 1, 6, PEERS)
    scatter_m = scatter_first(MID)
    start(scatter_m)
    compute(NEAR, -2, 0, 4, held=(MID, 1))
    arrive(scatter_f[2:] + scatter_f2)

    def far(n, carry):
        kv, r = n // ROWS, n % ROWS
        bsend[kv, r] = summed(FAR, kv, r).astype(jnp.bfloat16)
        return carry

    lax.fori_loop(0, 2 * ROWS, far, 0)
    back_first = remote(bsend, bmid, bz_send.at[0], bz_recv.at[0], (z_back, x))
    back_second = remote(msend, bfinal, bz_send.at[1], bz_recv.at[1], (z_back, x))
    back_first.start()
    compute(NEAR, -2, 4, 6)
    scatter_m2 = scatter_second(MID, scatter_m)
    start(scatter_m2)
    compute(NEAR, -2, 6, PEERS)
    scatter_a = scatter_first(NEAR)
    start(scatter_a)
    send_pair(NEAR, -2, PEERS // 2 - 1)
    arrive(scatter_m[2:] + scatter_m2)
    back_first.wait_recv()

    def middle(n, carry):
        kv, r = n // ROWS, n % ROWS
        msend[kv, r] = (summed(MID, kv, r) + bmid[kv, r].astype(jnp.float32)).astype(jnp.bfloat16)
        return carry

    lax.fori_loop(0, 2 * ROWS, middle, 0)
    back_second.start()
    scatter_a2 = scatter_second(NEAR, scatter_a)
    start(scatter_a2)

    def drain(which, e):
        def sent(n, carry):
            i = slot_of(which, e) + n
            pltpu.make_async_copy(obuf.at[i], rbuf.at[i], in_send.at[i]).wait()
            pltpu.make_async_copy(obuf.at[i], rbuf.at[i], out_send.at[i]).wait()
            return carry

        def came(n, carry):
            i = slot_of(which, e) + n
            pltpu.make_async_copy(obuf.at[i], rbuf.at[i], out_recv.at[i]).wait()
            return carry

        lax.fori_loop(1 if e == 0 else 0, PEERS, sent, 0)
        lax.fori_loop(0, PEERS, came, 0)

    drain(NEAR, 0)
    drain(NEAR, -1)
    arrive(scatter_a[2:] + scatter_a2)
    for which, e in ((MID, 0), (MID, -1), (FAR, 0), (FAR, 1)):
        drain(which, e)
    back_second.wait_recv()

    def near(n, carry):
        kv, r = n // ROWS, n % ROWS
        total = summed(NEAR, kv, r) + bfinal[kv, r].astype(jnp.float32)
        grad_ref[kv, r] = total.T.astype(jnp.bfloat16)
        return carry

    lax.fori_loop(0, 2 * ROWS, near, 0)

    for copy in (
        shift_first + shift_second + gather_a + gather_a2 + gather_m + gather_m2 + gather_f + gather_f2 + scatter_a
        + scatter_a2 + scatter_m + scatter_m2 + scatter_f + scatter_f2 + [back_first, back_second]
    ):
        copy.wait_send()
    drain(MID, 1)
    drain(NEAR, -2)


def settle(out_ref, grad_ref, attended_ref, query_ref, keys_ref, values_ref, rows, blocks, in_sem, out_sem):
    moves = []
    for m, dst in enumerate((attended_ref, query_ref)):
        for r in range(4):
            span = pl.ds(r * 32, 32)
            moves.append((out_ref.at[m, span], rows.at[m, span], dst.at[span]))
    for m, dst in enumerate((keys_ref, values_ref)):
        moves.append((grad_ref.at[m], blocks.at[m], dst))
    arriving = [pltpu.make_async_copy(src, mid, in_sem.at[n]) for n, (src, mid, _dst) in enumerate(moves)]
    leaving = [pltpu.make_async_copy(mid, dst, out_sem.at[n]) for n, (_src, mid, dst) in enumerate(moves)]
    for copy in arriving:
        copy.start()
    for first, second in zip(arriving, leaving):
        first.wait()
        second.start()
    for copy in leaving:
        copy.wait()


def on_device(queries, cotangent, cache_keys, cache_values, block_table, block_slot):
    seq = lax.axis_index("seq")
    z, y, c = seq // (YS * CS), (seq // CS) % YS, seq % CS
    flat = block_table[0].reshape(-1)
    blocks = block_slot.shape[0]
    hit = flat[:, None] == jnp.arange(blocks, dtype=jnp.int32)[None, :]
    rows = jnp.sum(jnp.where(hit, block_slot[None, :], 0), axis=1)
    item = jnp.arange(flat.shape[0], dtype=jnp.int32)
    src = item // 4
    away = ((src // PEERS - z) * (1 - 2 * c) + ZS) % ZS
    n = ((src % CS - c + CS) % CS) * YS + ((src // CS) % YS - y + YS) % YS
    slots = []
    for which in (NEAR, MID, FAR):
        slot = jnp.full_like(item, -1)
        for b, e in enumerate(OFFSETS[which]):
            slot = jnp.where(away == e % ZS, (BASE[which] + b * PEERS + n) * 4 + item % 4, slot)
        slots.append(slot)
    slot = jnp.stack(slots)
    same = (rows[:, None] == rows[None, :])[None] & (slot[:, None, :] < slot[:, :, None])
    before = jnp.max(jnp.where(same, slot[:, None, :], -1), axis=2)
    before = jnp.where(before < 0, ZERO, before).reshape(-1)
    owned = (rows[None, :] == jnp.arange(STORED, dtype=jnp.int32)[:, None])[None]
    final = jnp.max(jnp.where(owned, slot[:, None, :], -1), axis=2)
    final = jnp.where(final < 0, ZERO, final).reshape(-1)
    smem = pl.BlockSpec(memory_space=pltpu.SMEM)
    hbm = pl.BlockSpec(memory_space=pl.ANY)
    bf16 = jnp.bfloat16
    dma = pltpu.SemaphoreType.DMA
    out, grads = pl.pallas_call(
        kernel,
        out_shape=(
            jax.ShapeDtypeStruct((2, TOKENS, queries.shape[2]), bf16),
            jax.ShapeDtypeStruct((2, ROWS, NEIGH_LEN, HEAD_DIM), bf16),
        ),
        in_specs=[smem, smem, smem, hbm, hbm, hbm, hbm],
        out_specs=(hbm, pl.BlockSpec(memory_space=pltpu.VMEM)),
        scratch_shapes=[
            pltpu.VMEM((STEPS, 2, TOKENS, HEAD_DIM), bf16),
            pltpu.VMEM((STEPS, 2, TOKENS, HEAD_DIM), bf16),
            *[pltpu.VMEM((STORED, NEIGH_LEN, HEAD_DIM), bf16)] * 6,
            *[pltpu.VMEM((ZERO + 1, HEAD_DIM, NEIGH_LEN), jnp.float32)] * 2,
            pltpu.VMEM((3, XS, 2, ROWS, HEAD_DIM, NEIGH_LEN), bf16),
            *[pltpu.VMEM((3, 2, ROWS, HEAD_DIM, NEIGH_LEN), bf16)] * 3,
            *[pltpu.VMEM((2, ROWS, HEAD_DIM, NEIGH_LEN), bf16)] * 4,
            dma((STEPS,)), dma((STEPS,)), dma((STEPS,)), dma((STEPS,)),
            dma((2,)), dma((3, 3, 2)), dma((3, 3, 2)), dma((2, 2)), dma((2, 2)),
            dma((3, 3, 2)), dma((3, 3, 2)), dma((2,)), dma((2,)),
        ],
        compiler_params=pltpu.CompilerParams(
            collective_id=0, has_side_effects=True, vmem_limit_bytes=67043328
        ),
        name="retrieval_attention",
    )(rows, before, final, queries[0], cotangent[0], cache_keys, cache_values)
    attended, query_grad, keys_grad, values_grad = pl.pallas_call(
        settle,
        out_shape=(
            jax.ShapeDtypeStruct(out.shape[1:], bf16),
            jax.ShapeDtypeStruct(out.shape[1:], bf16),
            jax.ShapeDtypeStruct(grads.shape[1:], bf16),
            jax.ShapeDtypeStruct(grads.shape[1:], bf16),
        ),
        in_specs=[hbm, hbm],
        out_specs=(hbm,) * 4,
        scratch_shapes=[pltpu.VMEM(out.shape, bf16), pltpu.VMEM(grads.shape, bf16), dma((10,)), dma((10,))],
        compiler_params=pltpu.CompilerParams(vmem_limit_bytes=67043328),
        name="settle",
    )(out, grads)
    return attended[None], query_grad[None], keys_grad, values_grad


def solution(mesh):
    placed = (
        P("grp", "seq", None),
        P("grp", "seq", None),
        P("grp", None, "seq"),
        P("grp", None, "seq"),
        P("grp", None, None),
        P(),
    )
    return jax.shard_map(
        on_device,
        mesh=mesh,
        in_specs=placed,
        out_specs=(
            P("grp", "seq", None),
            P("grp", "seq", None),
            P("grp", None, "seq"),
            P("grp", None, "seq"),
        ),
        check_vma=False,
    )
```
